32 devices in a mesh: stream: 2 (over core), frames: 16 (over z, y, x).
Axes of the slice: x: 2, y: 2, z: 4, core: 2. Of those that a mesh axis runs over, the one named last changes fastest.
Arguments:
- tokens: bfloat16 [2048, 2, 1024], P('frames', 'stream'), may hold values from -6 to 6
- context: bfloat16 [2048, 4096], P('frames'), may hold values from -6 to 6
- w_in: bfloat16 [1024, 4096], P('stream', 'frames'), may hold values from -0.09375 to 0.09375
- attn_gain: bfloat16 [2, 1024], P('stream', 'frames'), may hold values from 0.5 to 1.5
- w_qkv: bfloat16 [2, 1024, 3072], P('stream', 'frames'), may hold values from -0.1875 to 0.1875
- w_out: bfloat16 [2, 1024, 1024], P('stream', 'frames'), may hold values from -0.1875 to 0.1875
- ffn_gain: bfloat16 [2, 1024], P('stream', 'frames'), may hold values from 0.5 to 1.5
- w_gate_up: bfloat16 [2, 1024, 5632], P('stream', 'frames'), may hold values from -0.1875 to 0.1875
- w_down: bfloat16 [2, 2816, 1024], P('stream', 'frames'), may hold values from -0.21875 to 0.21875
- cotangent: bfloat16 [2048, 2, 1024], P('frames', 'stream'), may hold values from -6 to 6
Outputs:
- out: float32 [2048, 2, 1024], P('frames', 'stream')
- grad_tokens: float32 [2048, 2, 1024], P('frames', 'stream')
- grad_context: float32 [2048, 4096], P('frames')
- grad_w_in: float32 [1024, 4096], P('stream', 'frames')
- grad_attn_gain: float32 [2, 1024], P('stream', 'frames')
- grad_w_qkv: float32 [2, 1024, 3072], P('stream', 'frames')
- grad_w_out: float32 [2, 1024, 1024], P('stream', 'frames')
- grad_ffn_gain: float32 [2, 1024], P('stream', 'frames')
- grad_w_gate_up: float32 [2, 1024, 5632], P('stream', 'frames')
- grad_w_down: float32 [2, 2816, 1024], P('stream', 'frames')
The draws below stay inside these ranges and needn't reach their ends.
All inputs are finite; a program needn't handle non-finite values.
Results may differ from the reference program's by a relative error of at most 0.014.
Values may be sent and summed in bfloat16 or wider, within the bound.
No kernel may reach another device: no remote copies, remote signals or barrier semaphores. Data moves between devices by JAX's collectives and lax.ppermute only.
A program may use at most 192 MiB of HBM per device.

```python
import math
import jax
import jax.numpy as jnp
from jax import lax

D = 1024
H = 16
HD = 64
FF = 2816
CTX = 4096
POS = 2
FRAMES = 2048


def block_scale(key, dims, shards, least, top_value):
    factor_of = 1.0
    for dim, parts in shards:
        heights = jax.random.uniform(jax.random.fold_in(jax.random.fold_in(key, 6), dim), (parts,), jnp.float32, least / len(shards), top_value / len(shards))
        factor_of = factor_of * jnp.repeat(jnp.exp(heights), dims[dim] // parts).reshape((-1,) + (1,) * (len(dims) - 1 - dim))
    return factor_of


def gaussian(key, shape, deviation, reach, pieces=(), dtype=jnp.bfloat16):
    values = jax.random.normal(key, shape, jnp.float32) * deviation
    if len(pieces) > 0:
        values = block_scale(key, shape, pieces, -0.22, 0.18) * values
    return jnp.clip(values, min=-reach, max=reach).astype(dtype)


def setup_inputs(seed: int = 0) -> dict:
    streams_of = jax.random.split(jax.random.key(seed), 11)
    tokens = gaussian(streams_of[0], (FRAMES, POS, D), 1.0, 6.0, ((0, 16), (1, 2)))
    context = gaussian(streams_of[1], (FRAMES, CTX), 1.0, 6.0, ((0, 16),))
    w_in = gaussian(streams_of[2], (D, CTX), CTX ** -0.5, 0.09375, ((0, 2), (1, 16)))
    attn_gain = jnp.clip(1.0 + 0.1 * jax.random.normal(streams_of[3], (POS, D), jnp.float32), 0.5, 1.5).astype(jnp.bfloat16)
    w_qkv = gaussian(streams_of[4], (POS, D, 3 * D), D ** -0.5, 0.1875, ((0, 2), (1, 16)))
    w_out = gaussian(streams_of[5], (POS, D, D), D ** -0.5, 0.1875, ((0, 2), (1, 16)))
    ffn_gain = jnp.clip(1.0 + 0.1 * jax.random.normal(streams_of[6], (POS, D), jnp.float32), 0.5, 1.5).astype(jnp.bfloat16)
    w_gate_up = gaussian(streams_of[7], (POS, D, 2 * FF), D ** -0.5, 0.1875, ((0, 2), (1, 16)))
    w_down = gaussian(streams_of[8], (POS, FF, D), (FF // 4) ** -0.5, 0.21875, ((0, 2), (1, 16)))
    cotangent = gaussian(streams_of[9], (FRAMES, POS, D), 1.0, 6.0, ((0, 16), (1, 2)))
    return {"tokens": tokens, "context": context, "w_in": w_in, "attn_gain": attn_gain, "w_qkv": w_qkv, "w_out": w_out, "ffn_gain": ffn_gain, "w_gate_up": w_gate_up, "w_down": w_down, "cotangent": cotangent}


@jax.custom_vjp
def low(v):
    return lax.optimization_barrier(v.astype(jnp.bfloat16)).astype(jnp.float32)

@jax.custom_vjp
def low_back(v):
    return v

def low_keep(v):
    return (low(v), None)

def low_pass(kept, grad):
    return (grad,)

def back_keep(v):
    return (v, None)

def back_low(kept, grad):
    return (low(grad),)
low.defvjp(low_keep, low_pass)
low_back.defvjp(back_keep, back_low)

def product(form, left, right):
    return jnp.einsum(form, left, right, precision=lax.Precision.HIGHEST)

def normalize(values):
    return values * lax.rsqrt(lax.optimization_barrier(jnp.mean(values * values, axis=-1, keepdims=True)) + 1e-05)

def forward(tokens, context, w_in, attn_gain, w_qkv, w_out, ffn_gain, w_gate_up, w_down):
    frame_count = tokens.shape[0]
    places = tokens.shape[1]
    projected = low_back(low(product('fc,dc->fd', context, w_in)))
    start = tokens + projected[:, None, :]
    normed_one = low(normalize(start) * attn_gain)
    qkv = low_back(low(product('fpd,pde->fpe', normed_one, w_qkv)))
    query = qkv[..., :D].reshape(frame_count, places, H, HD)
    keys = qkv[..., D:2 * D].reshape(frame_count, places, H, HD)
    values = qkv[..., 2 * D:].reshape(frame_count, places, H, HD)
    scores = product('fphe,fjhe->fhpj', query, keys) * HD ** (-0.5)
    allowed = jnp.arange(places)[:, None] >= jnp.arange(places)[None, :]
    scores = jnp.where(allowed, scores, -1e+30)
    weights = jax.nn.softmax(scores, axis=-1)
    mixed = low(product('fhpj,fjhe->fphe', weights, values).reshape(frame_count, places, D))
    middle = start + low_back(product('fpd,pde->fpe', mixed, w_out))
    normed_two = low(normalize(middle) * ffn_gain)
    gate_up = low_back(product('fpd,pde->fpe', normed_two, w_gate_up))
    hidden = low(jax.nn.silu(gate_up[..., :FF]) * gate_up[..., FF:])
    return middle + low_back(product('fpk,pkd->fpd', hidden, w_down))

def reference(tokens, context, w_in, attn_gain, w_qkv, w_out, ffn_gain, w_gate_up, w_down, cotangent):
    weights = tuple((item.astype(jnp.float32) for item in (w_in, attn_gain, w_qkv, w_out, ffn_gain, w_gate_up, w_down)))
    block = math.gcd(FRAMES, 2048)
    blocks = FRAMES // block
    token_blocks = tokens.astype(jnp.float32).reshape(blocks, block, POS, D)
    context_blocks = context.astype(jnp.float32).reshape(blocks, block, CTX)
    cot_blocks = cotangent.astype(jnp.float32).reshape(blocks, block, POS, D)

    def step(carry, inputs):
        token_part, context_part, cot_part = inputs
        result, pull = jax.vjp(forward, token_part, context_part, *weights)
        grads = pull(cot_part)
        carry = tuple((total + piece for total, piece in zip(carry, grads[2:])))
        return (carry, (result, grads[0], grads[1]))
    start_carry = tuple((jnp.zeros(item.shape, jnp.float32) for item in weights))
    totals, stacked = lax.scan(step, start_carry, (token_blocks, context_blocks, cot_blocks))
    result = stacked[0].reshape(FRAMES, POS, D)
    grad_tokens = stacked[1].reshape(FRAMES, POS, D)
    grad_context = stacked[2].reshape(FRAMES, CTX)
    return (result, grad_tokens, grad_context, totals[0], totals[1], totals[2], totals[3], totals[4], totals[5], totals[6])
```

```python
import jax
import jax.numpy as jnp
from jax import lax
from jax.sharding import Mesh
from jax.sharding import PartitionSpec as P

HD = 64
F32 = jnp.float32
BF = jnp.bfloat16


def dot(form, a, b):
    return jnp.einsum(form, a, b, preferred_element_type=F32)


def peers(r):
    return [(i, i ^ r) for i in range(4)]


def hop(x, r):
    return lax.ppermute(x, "t", peers(r))


def spread(x):
    return [x] + [hop(x, r) for r in (1, 2, 3)]


def collect(x):
    b = x.shape[0] // 4
    low = [x[r * b : (r + 1) * b].astype(BF) for r in range(4)]
    return low[0].astype(F32) + sum(hop(low[r], r).astype(F32) for r in (1, 2, 3))


def swap(x):
    return lax.ppermute(x, "stream", [(0, 1), (1, 0)])


def norm_parts(v):
    scale = lax.rsqrt(jnp.mean(v * v, axis=-1, keepdims=True) + 1e-05)
    return v * scale, scale


def norm_back(unit, scale, g):
    return scale * (g - unit * jnp.mean(g * unit, axis=-1, keepdims=True))


def columns_to_t(w, k):
    rows = w.shape[0]
    c = w.shape[1] // (k * 16)
    w = w.reshape(rows, k, 4, 4, c).transpose(3, 0, 1, 2, 4).reshape(4, rows, k * 4 * c)
    return lax.all_to_all(w, "t", 0, 0, tiled=True).reshape(4 * rows, k * 4 * c)


def columns_back(g, k):
    rows = g.shape[0] // 4
    c = g.shape[1] // (k * 4)
    g = lax.all_to_all(g.reshape(4, rows, k * 4 * c), "t", 0, 0, tiled=True)
    return g.reshape(4, rows, k, 4, c).transpose(1, 2, 3, 0, 4).reshape(rows, k * 16 * c)


def on_device(
    tokens, context, w_in, attn_gain, w_qkv, w_out, ffn_gain, w_gate_up, w_down, cotangent
):
    s = lax.axis_index("stream")
    t = lax.axis_index("t")
    many = lax.axis_size("d2") > 1
    frames = tokens.shape[0]
    d = tokens.shape[2]
    half = frames // 2

    def near(w, axis=0):
        return lax.all_gather(w, "d2", axis=axis, tiled=True) if many else w

    def near_sum(g, axis=0):
        return lax.psum_scatter(g, "d2", scatter_dimension=axis, tiled=True) if many else g

    def over_d(w, axis=0):
        return lax.all_gather(w, "d1", axis=axis, tiled=True)

    def sum_d(g, axis=0):
        return lax.psum_scatter(g.astype(BF), "d1", scatter_dimension=axis, tiled=True)

    tokens = tokens[:, 0]
    cotangent = cotangent[:, 0]
    gain_one = lax.all_gather(attn_gain[0], ("d1", "t", "d2"), axis=0, tiled=True).astype(F32)
    gain_two = lax.all_gather(ffn_gain[0], ("d1", "t", "d2"), axis=0, tiled=True).astype(F32)
    in_w = over_d(near(w_in, 1), 1)
    qkv_w = over_d(columns_to_t(near(w_qkv[0]), 3))
    out_w = over_d(near(w_out[0]))
    gu_w = over_d(columns_to_t(near(w_gate_up[0]), 2))
    down_w = over_d(near(w_down[0]))

    mine = lax.dynamic_slice_in_dim(context, s * half, half, 0).reshape(half, 4, 4, -1)
    feats = mine.shape[-1] * 4
    parts = []
    for r in range(4):
        block = lax.dynamic_index_in_dim(mine, t ^ r, 2, keepdims=False).reshape(half, feats)
        parts.append(hop(block, r) if r else block)
    own = jnp.stack(parts)
    other = swap(own)
    group = jnp.where(
        s == 0, jnp.concatenate([own, other], axis=1), jnp.concatenate([other, own], axis=1)
    ).reshape(4 * frames, feats)

    proj_half = collect(dot("fc,dc->fd", group, in_w)).astype(BF)
    proj_other = swap(proj_half)
    projected = jnp.where(
        s == 0,
        jnp.concatenate([proj_half, proj_other], axis=1),
        jnp.concatenate([proj_other, proj_half], axis=1),
    )
    start = tokens.astype(F32) + projected.astype(F32)
    unit_one, scale_one = norm_parts(start)
    normed_one = jnp.concatenate(spread((unit_one * gain_one).astype(BF)))
    qkv = dot("fd,de->fe", normed_one, qkv_w).astype(BF)
    width = qkv.shape[1] // 3
    far = lax.ppermute(qkv[:, width:], "stream", [(0, 1)]).astype(F32)
    q, k, v = (qkv[:, i * width : (i + 1) * width].astype(F32) for i in range(3))
    lane = jnp.arange(width) // HD
    heads = (lane[:, None] == lane[None, :]).astype(F32)

    def head_sum(x):
        return jnp.dot(x, heads, precision=lax.Precision.HIGHEST)

    dk = k - far[:, :width]
    dv = v - far[:, width:]
    w_own = jnp.where(s == 0, 1.0, jax.nn.sigmoid(head_sum(q * dk) * HD ** (-0.5)))
    w_far = 1.0 - w_own
    mixed = (w_own * v + w_far * far[:, width:]).astype(BF)
    middle = start + collect(dot("fd,de->fe", mixed, out_w))
    unit_two, scale_two = norm_parts(middle)
    normed_two = jnp.concatenate(spread((unit_two * gain_two).astype(BF)))
    cot = jnp.concatenate(spread(cotangent))
    gate_up = dot("fd,de->fe", normed_two, gu_w)
    ff = gate_up.shape[1] // 2
    gate, up = gate_up[:, :ff], gate_up[:, ff:]
    sig = jax.nn.sigmoid(gate)
    hidden = (gate * sig * up).astype(BF)
    result = middle + collect(dot("fk,kd->fd", hidden, down_w))

    grad_down = near_sum(sum_d(dot("fk,fd->kd", hidden, cot)).astype(F32))
    grad_hidden = dot("fd,kd->fk", cot, down_w)
    grad_gu = jnp.concatenate(
        [grad_hidden * up * sig * (1.0 + gate * (1.0 - sig)), grad_hidden * gate * sig], axis=-1
    ).astype(BF)
    grad_normed_two = collect(dot("fe,de->fd", grad_gu, gu_w))
    grad_gate_up = near_sum(
        columns_back(sum_d(dot("fd,fe->de", normed_two, grad_gu)), 2).astype(F32)
    )
    grad_gain_two = jnp.sum(grad_normed_two * unit_two, axis=0)
    grad_middle = cotangent.astype(F32) + norm_back(
        unit_two, scale_two, grad_normed_two * gain_two
    )
    branch = jnp.concatenate(spread(grad_middle.astype(BF)))
    grad_out = near_sum(sum_d(dot("fd,fe->de", mixed, branch)).astype(F32))
    gm = dot("fe,de->fd", branch, out_w)
    gs = w_own * w_far * head_sum(gm * dv) * HD ** (-0.5)
    gq = gs * dk
    gk = gs * q
    back = lax.ppermute(
        jnp.concatenate([-gk, w_far * gm], axis=1).astype(BF), "stream", [(1, 0)]
    ).astype(F32)
    grad_kv = jnp.concatenate([gk, w_own * gm], axis=1) + back
    grad_qkv_low = jnp.concatenate([gq, grad_kv], axis=1).astype(BF)
    grad_normed_one = collect(dot("fe,de->fd", grad_qkv_low, qkv_w))
    grad_qkv = near_sum(
        columns_back(sum_d(dot("fd,fe->de", normed_one, grad_qkv_low)), 3).astype(F32)
    )
    grad_gain_one = jnp.sum(grad_normed_one * unit_one, axis=0)
    grad_start = grad_middle + norm_back(unit_one, scale_one, grad_normed_one * gain_one)
    halves = grad_start.astype(BF).reshape(frames, 2, d // 2)
    keep = lax.dynamic_index_in_dim(halves, s, 1, keepdims=False)
    give = lax.dynamic_index_in_dim(halves, 1 - s, 1, keepdims=False)
    grad_proj = (keep.astype(F32) + swap(give).astype(F32)).astype(BF)
    gproj = jnp.concatenate(spread(grad_proj))
    grad_in = near_sum(sum_d(dot("fd,fc->dc", gproj, group), 1).astype(F32), 1)
    term = dot("fd,dc->fc", gproj, in_w).astype(BF).reshape(4, 2, half, feats)
    keep = lax.dynamic_index_in_dim(term, s, 1, keepdims=False)
    give = lax.dynamic_index_in_dim(term, 1 - s, 1, keepdims=False)
    both = (keep.astype(F32) + swap(give).astype(F32)).astype(BF).reshape(4, half, 4, feats // 4)
    got = jnp.stack([hop(both[r], r) if r else both[0] for r in range(4)])
    ordered = jnp.stack(
        [lax.dynamic_index_in_dim(got, t ^ j, 0, keepdims=False) for j in range(4)], axis=2
    ).reshape(half, -1)
    far_half = swap(ordered)
    grad_context = jnp.where(
        s == 0, jnp.concatenate([ordered, far_half]), jnp.concatenate([far_half, ordered])
    ).astype(F32)
    gains = lax.psum_scatter(
        jnp.stack([grad_gain_one, grad_gain_two]),
        ("d1", "t", "d2"),
        scatter_dimension=1,
        tiled=True,
    )
    return (
        result[:, None],
        grad_start[:, None],
        grad_context,
        grad_in,
        gains[:1],
        grad_qkv[None],
        grad_out[None],
        gains[1:],
        grad_gate_up[None],
        grad_down[None],
    )


def solution(mesh):
    n = mesh.shape["frames"]
    grid = Mesh(mesh.devices.reshape(2, 4, 4, n // 16), ("stream", "d1", "t", "d2"))
    f = ("d1", "t", "d2")
    return jax.shard_map(
        on_device,
        mesh=grid,
        in_specs=(
            P(f, "stream", None),
            P(f, None),
            P("stream", f),
            P("stream", f),
            P("stream", f, None),
            P("stream", f, None),
            P("stream", f),
            P("stream", f, None),
            P("stream", f, None),
            P(f, "stream", None),
        ),
        out_specs=(
            P(f, "stream", None),
            P(f, "stream", None),
            P(f, None),
            P("stream", f),
            P("stream", f),
            P("stream", f, None),
            P("stream", f, None),
            P("stream", f),
            P("stream", f, None),
            P("stream", f, None),
        ),
        check_vma=False,
    )
```

```python
import jax
import jax.numpy as jnp
from jax import lax
from jax.experimental import pallas as pl
from jax.experimental.pallas import tpu as pltpu
from jax.sharding import Mesh
from jax.sharding import PartitionSpec as P

HD = 64
F32 = jnp.float32
BF = jnp.bfloat16


def dot(form, a, b):
    return jnp.einsum(form, a, b, preferred_element_type=F32)


def peers(r):
    return [(i, i ^ r) for i in range(4)]


def hop(x, r):
    return lax.ppermute(x, "t", peers(r))


def spread(x):
    a, b = hop(x, 1), hop(x, 2)
    return [x, a, b, hop(b, 1)]


def zhop(x, r):
    return lax.ppermute(x, "d1", peers(r))


def gather_z(w):
    a, b = zhop(w, 1), zhop(w, 3)
    return [w, a, zhop(b, 1), b]


def scatter_z(g):
    g = [x.astype(BF) for x in g]
    far = (g[3].astype(F32) + zhop(g[2], 1).astype(F32)).astype(BF)
    return g[0].astype(F32) + zhop(g[1], 1).astype(F32) + zhop(far, 3).astype(F32)


def total(parts):
    return sum(p.astype(F32) for p in parts)


def turn(x, d, axis):
    n = x.shape[axis] // 4
    return [lax.dynamic_slice_in_dim(x, (d ^ r) * n, n, axis) for r in range(4)]


def collect(x):
    b = x.shape[0] // 4
    low = [x[r * b : (r + 1) * b].astype(BF) for r in range(4)]
    return low[0].astype(F32) + sum(hop(low[r], r).astype(F32) for r in (3, 2, 1))


def swap(x):
    return lax.ppermute(x, "stream", [(0, 1), (1, 0)])


def norm_parts(v):
    scale = lax.rsqrt(jnp.mean(v * v, axis=-1, keepdims=True) + 1e-05)
    return v * scale, scale


def norm_back(unit, scale, g):
    return scale * (g - unit * jnp.mean(g * unit, axis=-1, keepdims=True))


def quarters(x, axis=0):
    n = x.shape[axis] // 4
    return [lax.slice_in_dim(x, r * n, (r + 1) * n, axis=axis) for r in range(4)]


def tie(x, *after):
    return lax.optimization_barrier((x,) + after)[0]


def call(body, outs, *args, scalars=None):
    inside = [pl.BlockSpec(memory_space=pltpu.VMEM)] * len(args)
    if scalars is not None:
        inside = [pl.BlockSpec(memory_space=pltpu.SMEM)] + inside
        args = (scalars,) + args
    single = not isinstance(outs, list)
    shapes = [jax.ShapeDtypeStruct(*o) for o in ([outs] if single else outs)]
    got = pl.pallas_call(
        body,
        out_shape=shapes,
        in_specs=inside,
        out_specs=[pl.BlockSpec(memory_space=pltpu.VMEM)] * len(shapes),
        compiler_params=pltpu.CompilerParams(vmem_limit_bytes=48 << 20),
    )(*args)
    return got[0] if single else got


def join(blocks, d=None):
    n, c = blocks[0].shape

    def body(*refs):
        shift = 0 if d is None else refs[0][0]
        ins = refs if d is None else refs[1:]
        for r in range(4):
            row = r * n if d is None else pl.multiple_of((shift ^ r) * n, 16)
            ins[4][pl.ds(row, n)] = ins[r][...]

    scalars = None if d is None else d.astype(jnp.int32)[None]
    return call(body, ((4 * n, c), blocks[0].dtype), *blocks, scalars=scalars)


def beside(blocks, rows):
    c = blocks[0].shape[1]

    def body(*refs):
        for r in range(4):
            refs[4][:, r * c : (r + 1) * c] = refs[r][:rows]

    return call(body, ((rows, 4 * c), blocks[0].dtype), *blocks)


def pack_columns(w, k):
    rows = w.shape[0]
    c = w.shape[1] // (k * 16)

    def body(w_ref, o_ref):
        x = w_ref[...]
        for t in range(4):
            o_ref[t] = jnp.concatenate(
                [x[:, (i * 4 + t) * c : (i * 4 + t + 1) * c] for i in range(k * 4)], axis=1
            )

    return call(body, ((4, rows, k * 4 * c), w.dtype), w)


def unpack_columns(g, k):
    rows = g.shape[1]
    c = g.shape[2] // (k * 4)

    def body(g_ref, o_ref):
        x = [g_ref[t].astype(F32) for t in range(4)]
        o_ref[...] = jnp.concatenate(
            [x[t][:, i * c : (i + 1) * c] for i in range(k * 4) for t in range(4)], axis=1
        )

    return call(body, ((rows, k * 16 * c), F32), g)


def pack_context(context, scalars):
    half = context.shape[0] // 2
    c = context.shape[1] // 16

    def body(n_ref, x_ref, *o_refs):
        s, t, d = n_ref[0], n_ref[1], n_ref[2]
        for r in range(4):
            for q in range(4):
                col = pl.multiple_of(((d ^ q) * 4 + (t ^ r)) * c, c)
                row = pl.multiple_of(s * half, half)
                o_refs[r][:, q * c : (q + 1) * c] = x_ref[pl.ds(row, half), pl.ds(col, c)]

    return call(body, [((half, 4 * c), context.dtype)] * 4, context, scalars=scalars)


def unpack_context(own, other, scalars):
    half = own.shape[1]
    c = own.shape[2] // 4

    def body(n_ref, a_ref, b_ref, o_ref):
        s, t, d = n_ref[0], n_ref[1], n_ref[2]
        for ref, place in ((a_ref, s), (b_ref, 1 - s)):
            row = pl.multiple_of(place * half, half)
            for r in range(4):
                for q in range(4):
                    col = pl.multiple_of(((d ^ q) * 4 + (t ^ r)) * c, c)
                    o_ref[pl.ds(row, half), pl.ds(col, c)] = ref[
                        r, :, q * c : (q + 1) * c
                    ].astype(F32)

    return call(body, ((2 * half, 16 * c), F32), own, other, scalars=scalars)


def on_device(
    tokens, context, w_in, attn_gain, w_qkv, w_out, ffn_gain, w_gate_up, w_down, cotangent
):
    s = lax.axis_index("stream")
    t = lax.axis_index("t")
    d = lax.axis_index("d1")
    many = lax.axis_size("d2") > 1
    frames = tokens.shape[0]
    wide = tokens.shape[2]
    half = frames // 2

    def near(w, axis=0):
        return lax.all_gather(w, "d2", axis=axis, tiled=True) if many else w

    def near_sum(g, axis=0):
        return lax.psum_scatter(g, "d2", scatter_dimension=axis, tiled=True) if many else g

    scalars = jnp.stack([s, t, d]).astype(jnp.int32)

    def over_d(w):
        return lax.all_gather(w, "d1", axis=0, tiled=True)

    def sum_d(g):
        return lax.psum_scatter(g.astype(BF), "d1", scatter_dimension=0, tiled=True).astype(F32)

    tokens = tokens[:, 0]
    cotangent = cotangent[:, 0]
    every = ("d1", "t", "d2")

    each = attn_gain.shape[1]
    gains = jnp.concatenate(
        [
            lax.all_gather(g[0], "d2", axis=0, tiled=True) if many else g[0]
            for g in (attn_gain, ffn_gain)
        ]
    )
    some = gains.shape[0]
    in_mine = near(w_in, 1)
    in_mine = jnp.concatenate(
        [in_mine, jnp.pad(gains[None], ((0, 15), (0, in_mine.shape[1] - some)))]
    )
    in_one, in_three = zhop(in_mine, 1), zhop(in_mine, 3)
    parts = pack_context(context, scalars)
    feats = parts[0].shape[1]
    got = {r: hop(parts[r], r) for r in (3, 2, 1)}
    packed = pack_columns(tie(near(w_qkv[0]), parts[0]), 3)
    qkv_mine = lax.all_to_all(packed, "t", 0, 0, tiled=True).reshape(-1, packed.shape[2])
    packed = pack_columns(tie(near(w_gate_up[0]), qkv_mine), 2)
    gu_mine = lax.all_to_all(packed, "t", 0, 0, tiled=True).reshape(-1, packed.shape[2])
    own = tie(jnp.stack([parts[0], got[1], got[2], got[3]]), qkv_mine)
    other = swap(own)
    in_two = zhop(tie(in_three, own), 1)
    qkv_one, qkv_three = zhop(qkv_mine, 1), zhop(qkv_mine, 3)
    group = jnp.where(
        s == 0, jnp.concatenate([own, other], axis=1), jnp.concatenate([other, own], axis=1)
    ).reshape(4 * frames, feats)
    in_w = beside([in_mine, in_one, in_two, in_three], near(w_in, 1).shape[0])
    partial = dot("fc,dc->fd", group, in_w).astype(BF)

    gains = jnp.concatenate([w[-16:, :some] for w in (in_mine, in_one, in_two, in_three)], axis=1)
    size = partial.shape[0] // 4
    parts = [jnp.concatenate([partial[r * size : (r + 1) * size], gains]) for r in range(4)]
    parts = [parts[0]] + [hop(parts[r], r) for r in (3, 2, 1)]
    proj_half = total([w[:size] for w in parts]).astype(BF)
    proj_half = tie(proj_half, gu_mine, qkv_one, qkv_three)
    qkv_two = zhop(tie(qkv_three, proj_half), 1)
    out_mine = tie(near(w_out[0]), proj_half)
    out_one, out_three = zhop(out_mine, 1), zhop(out_mine, 3)
    gains = jnp.stack([parts[i][size].astype(F32) for i in (0, 3, 2, 1)])
    gains = jnp.stack([lax.dynamic_index_in_dim(gains, t ^ r, 0, keepdims=False) for r in range(4)])
    gains = gains.reshape(4, 4, 2, some // 2).transpose(2, 1, 0, 3).reshape(2, wide)
    gain_one, gain_two = (jnp.concatenate(turn(gains[i], d, 0)) for i in (0, 1))
    proj_other = swap(proj_half)
    projected = jnp.where(
        s == 0,
        jnp.concatenate([proj_half, proj_other], axis=1),
        jnp.concatenate([proj_other, proj_half], axis=1),
    )
    start = tokens.astype(F32) + projected.astype(F32)
    unit_one, scale_one = norm_parts(start)
    mine = jnp.concatenate(turn((unit_one * gain_one).astype(BF), d, 1), axis=1)
    by_x, by_y = hop(mine, 1), hop(mine, 2)
    by_xy = hop(tie(by_y, qkv_two), 1)
    gu_mine = tie(gu_mine, mine)
    gu_one, gu_three = zhop(gu_mine, 1), zhop(gu_mine, 3)
    normed_one = tie(join([mine, by_x, by_y, by_xy]), out_one, out_three)
    out_two = zhop(out_three, 1)
    qkv_w = join([qkv_mine, qkv_one, qkv_two, qkv_three])
    out_w = join([out_mine, out_one, out_two, out_three], d)
    qkv = dot("fd,de->fe", normed_one, qkv_w).astype(BF)
    width = qkv.shape[1] // 3
    far = lax.ppermute(qkv[:, width:], "stream", [(0, 1)])
    far = far.astype(F32)
    q, k, v = (qkv[:, i * width : (i + 1) * width].astype(F32) for i in range(3))
    lane = jnp.arange(width) // HD
    heads = (lane[:, None] == lane[None, :]).astype(F32)

    def head_sum(x):
        return jnp.dot(x, heads, precision=lax.Precision.HIGHEST)

    dk = k - far[:, :width]
    dv = v - far[:, width:]
    w_own = jnp.where(s == 0, 1.0, jax.nn.sigmoid(head_sum(q * dk) * HD ** (-0.5)))
    w_far = 1.0 - w_own
    mixed = (w_own * v + w_far * far[:, width:]).astype(BF)
    mixed = tie(mixed, gu_one)
    partial = dot("fd,de->fe", mixed, out_w).astype(BF)
    cot = lax.all_to_all(
        jnp.broadcast_to(tie(cotangent, partial)[None], (4, frames, wide)), "t", 0, 0, tiled=True
    )
    down_mine = near(w_down[0])
    down_one = zhop(tie(down_mine, normed_one), 1)
    middle = start + tie(collect(partial), gu_three, down_one)

    unit_two, scale_two = norm_parts(middle)
    mine = jnp.concatenate(turn((unit_two * gain_two).astype(BF), d, 1), axis=1)
    by_x, by_y = hop(mine, 1), hop(mine, 2)
    gu_two = zhop(gu_three, 1)
    by_xy = hop(by_y, 1)
    down_three = zhop(tie(down_mine, middle), 3)
    normed_two = tie(join([mine, by_x, by_y, by_xy]), down_three)
    gu_w = join([gu_mine, gu_one, gu_two, gu_three])
    cot = jnp.concatenate(turn(cot.reshape(4 * frames, wide), t, 0))
    gate_up = dot("fd,de->fe", normed_two, gu_w)
    down_two = zhop(down_three, 1)
    down_w = join([down_mine, down_one, down_two, down_three], d)
    ff = gate_up.shape[1] // 2
    gate, up = gate_up[:, :ff], gate_up[:, ff:]
    sig = jax.nn.sigmoid(gate)
    hidden = (gate * sig * up).astype(BF)
    g = turn(dot("fk,fd->kd", hidden, cot).astype(BF), d, 0)
    down_back_two, down_back_one = zhop(g[2], 1), zhop(g[1], 1)
    grad_hidden = dot("fd,kd->fk", tie(cot, g[0]), down_w)
    grad_gu = jnp.concatenate(
        [grad_hidden * up * sig * (1.0 + gate * (1.0 - sig)), grad_hidden * gate * sig], axis=-1
    ).astype(BF)
    partial = dot("fe,de->fd", grad_gu, gu_w).astype(BF)
    grad_normed_two = jnp.concatenate(turn(tie(collect(partial), down_back_two), d, 1), axis=1)
    u = quarters(dot("fd,fe->de", normed_two, tie(grad_gu, partial)).astype(BF))
    gu_two = zhop(u[2], 1)
    far_sum = (g[3].astype(F32) + tie(down_back_two, grad_normed_two).astype(F32)).astype(BF)
    down_three = zhop(far_sum, 3)
    grad_gain_two = jnp.sum(grad_normed_two * unit_two, axis=0)
    grad_middle = cotangent.astype(F32) + norm_back(
        unit_two, scale_two, grad_normed_two * gain_two
    )
    mine = tie(grad_middle.astype(BF), far_sum)
    by_x, by_y = hop(mine, 1), hop(mine, 2)
    gu_one = zhop(tie(u[1], mine), 1)
    by_xy = hop(by_y, 1)
    branch = tie(join([mine, by_x, by_y, by_xy]), gu_two)
    grad_down = near_sum(
        g[0].astype(F32) + down_back_one.astype(F32) + tie(down_three, branch).astype(F32)
    )

    gm = dot("fe,de->fd", branch, out_w)
    gs = w_own * w_far * head_sum(gm * dv) * HD ** (-0.5)
    gq = gs * dk
    gk = gs * q
    back = lax.ppermute(
        jnp.concatenate([-gk, w_far * gm], axis=1).astype(BF), "stream", [(1, 0)]
    ).astype(F32)
    grad_kv = jnp.concatenate([gk, w_own * gm], axis=1) + back
    far_sum = (u[3].astype(F32) + tie(gu_two, branch).astype(F32)).astype(BF)
    gu_three = zhop(far_sum, 3)
    grad_qkv_low = jnp.concatenate([gq, grad_kv], axis=1).astype(BF)
    grad_qkv_low = tie(grad_qkv_low, far_sum, gu_one)
    partial = dot("fe,de->fd", grad_qkv_low, qkv_w).astype(BF)
    grad_normed_one = jnp.concatenate(turn(collect(partial), d, 1), axis=1)
    g = quarters(dot("fd,fe->de", normed_one, tie(grad_qkv_low, partial)).astype(BF))
    h = turn(dot("fd,fe->de", tie(mixed, g[0]), branch).astype(BF), d, 0)
    grad_gain_one = jnp.sum(grad_normed_one * unit_one, axis=0)
    grad_start = grad_middle + norm_back(unit_one, scale_one, grad_normed_one * gain_one)
    halves = grad_start.astype(BF).reshape(frames, 2, wide // 2)
    keep = lax.dynamic_index_in_dim(halves, s, 1, keepdims=False)
    give = lax.dynamic_index_in_dim(halves, 1 - s, 1, keepdims=False)
    grad_proj = (keep.astype(F32) + swap(give).astype(F32)).astype(BF)
    by_x, by_y = hop(grad_proj, 1), hop(grad_proj, 2)
    qkv_back_two = zhop(g[2], 1)
    qkv_back_one = zhop(tie(g[1], grad_proj), 1)
    by_xy = hop(by_y, 1)
    gproj = join([grad_proj, by_x, by_y, by_xy])
    gu_sum = u[0].astype(F32) + gu_one.astype(F32) + tie(gu_three, gproj).astype(F32)
    far_sum = (g[3].astype(F32) + tie(qkv_back_two, gproj).astype(F32)).astype(BF)
    qkv_back_three = zhop(far_sum, 3)
    result = middle + collect(dot("fk,kd->fd", tie(hidden, gproj), down_w).astype(BF))
    out_back_two, out_back_one = zhop(tie(h[2], result), 1), zhop(tie(h[1], result), 1)

    term = dot("fd,dc->fc", gproj, in_w).astype(BF).reshape(4, 2, half, feats)
    keep = lax.dynamic_index_in_dim(term, s, 1, keepdims=False)
    give = lax.dynamic_index_in_dim(term, 1 - s, 1, keepdims=False)
    both = (keep.astype(F32) + swap(give).astype(F32)).astype(BF)
    g_in = quarters(dot("fd,fc->dc", gproj, tie(group, give)).astype(BF), 1)
    got = {r: hop(both[r], r) for r in (3, 2, 1)}
    in_back_two = zhop(tie(g_in[2], both), 1)
    grad_qkv = g[0].astype(F32) + qkv_back_one.astype(F32) + qkv_back_three.astype(F32)
    gu_back = lax.all_to_all(
        tie(gu_sum.astype(BF), both).reshape(4, -1, gu_sum.shape[1]), "t", 0, 0, tiled=True
    )
    qkv_back = lax.all_to_all(
        tie(grad_qkv.astype(BF), gu_back).reshape(4, -1, grad_qkv.shape[1]), "t", 0, 0, tiled=True
    )
    far_sum = (h[3].astype(F32) + out_back_two.astype(F32)).astype(BF)
    out_back_three = zhop(far_sum, 3)
    grad_out = near_sum(
        h[0].astype(F32) + out_back_one.astype(F32) + out_back_three.astype(F32)
    )
    got = jnp.stack([both[0], got[1], got[2], got[3]])
    far_sum = (g_in[3].astype(F32) + tie(in_back_two, got).astype(F32)).astype(BF)
    in_back_three, in_back_one = zhop(far_sum, 3), zhop(tie(g_in[1], got), 1)
    grad_context = unpack_context(got, swap(got), scalars)
    grad_gate_up = near_sum(unpack_columns(gu_back, 2))
    grad_qkv = near_sum(unpack_columns(qkv_back, 3))
    grad_in = near_sum(
        g_in[0].astype(F32) + in_back_one.astype(F32) + in_back_three.astype(F32), 1
    )
    gains = jnp.stack([grad_gain_one, grad_gain_two]).reshape(2, -1, each).transpose(1, 0, 2)
    gains = jnp.sum(lax.all_to_all(tie(gains, both), every, 0, 0, tiled=True), axis=0)
    return (
        result[:, None],
        grad_start[:, None],
        grad_context,
        grad_in,
        gains[:1],
        grad_qkv[None],
        grad_out[None],
        gains[1:],
        grad_gate_up[None],
        grad_down[None],
    )


def solution(mesh):
    n = mesh.shape["frames"]
    grid = Mesh(mesh.devices.reshape(2, 4, 4, n // 16), ("stream", "d1", "t", "d2"))
    f = ("d1", "t", "d2")
    return jax.shard_map(
        on_device,
        mesh=grid,
        in_specs=(
            P(f, "stream", None),
            P(f, None),
            P("stream", f),
            P("stream", f),
            P("stream", f, None),
            P("stream", f, None),
            P("stream", f),
            P("stream", f, None),
            P("stream", f, None),
            P(f, "stream", None),
        ),
        out_specs=(
            P(f, "stream", None),
            P(f, "stream", None),
            P(f, None),
            P("stream", f),
            P("stream", f),
            P("stream", f, None),
            P("stream", f, None),
            P("stream", f),
            P("stream", f, None),
            P("stream", f, None),
        ),
        check_vma=False,
    )
```

```python
import jax
import jax.numpy as jnp
from jax import lax
from jax.experimental import pallas as pl
from jax.experimental.pallas import tpu as pltpu
from jax.sharding import Mesh
from jax.sharding import PartitionSpec as P

HD = 64
F32 = jnp.float32
BF = jnp.bfloat16
NN = (((1,), (0,)), ((), ()))
NT = (((1,), (1,)), ((), ()))
TN = (((0,), (0,)), ((), ()))


def mm(a, b, form=NN):
    return lax.dot_general(a, b, form, preferred_element_type=F32)


DUE = {
    "gu": "half",
    "qkv3": "half",
    "qkv1": "mine1",
    "qkv2": "byy1",
    "up3": "kv",
    "gu1": "byxy1",
    "cot": "parts1",
    "low3": "mid",
    "up2": "byy2",
    "down1": "byy2",
    "g1": "nb2",
    "g2": "branch",
    "u1": "parts3",
    "result": "into",
    "h1": "gpy",
    "u2": "gproj",
    "in1": "got",
    "u3": "both",
    "h2": "got",
    "h3": "gu_out",
    "in2": "gu_out",
    "down3": "hidden",
    "g3": "context",
}
SKIP = (6, 7, 23, 32, 36)
COST = {
    "": 3.0,
    "unpack_columns": 10.0,
    "row_parts": 10.0,
    "pack_pairs": 0.3,
}


def tie(x, *after):
    return lax.optimization_barrier((x,) + after)[0]


def opt(i, x, *after):
    return x if i in SKIP else tie(x, *after)


def corner(i, by_y, x):
    return hop(by_y, 1) if i not in SKIP else hop(x, 3)


class Flying(dict):
    def due(self, point, x):
        after = [v for k, v in self.items() if DUE.get(k) == point]
        return tie(x, *after) if after else x


def hop(x, r):
    return lax.ppermute(x, "t", [(i, i ^ r) for i in range(4)])


def zhop(x, r):
    return lax.ppermute(x, "d1", [(i, i ^ r) for i in range(4)])


def inward(x):
    return lax.ppermute(x, "d1", [(0, 1), (3, 2)])


def across(x):
    return lax.ppermute(x, "d1", [(1, 2), (2, 1)])


def swap(x):
    return lax.ppermute(x, "stream", [(0, 1), (1, 0)])


def collect(parts):
    return [parts[0]] + [hop(parts[r], r) for r in (1, 2, 3)]


def call(body, outs, *args, scalars=None, scratch=()):
    inside = [pl.BlockSpec(memory_space=pltpu.VMEM)] * len(args)
    if scalars is not None:
        inside = [pl.BlockSpec(memory_space=pltpu.SMEM)] + inside
        args = (scalars,) + args
    single = not isinstance(outs, list)
    shapes = [jax.ShapeDtypeStruct(*o) for o in ([outs] if single else outs)]
    got = pl.pallas_call(
        body,
        out_shape=shapes,
        in_specs=inside,
        out_specs=[pl.BlockSpec(memory_space=pltpu.VMEM)] * len(shapes),
        scratch_shapes=[pltpu.VMEM(*x) for x in scratch],
        compiler_params=pltpu.CompilerParams(vmem_limit_bytes=24 << 20),
        cost_estimate=pl.CostEstimate(
            flops=int(COST.get(body.__qualname__.split(".")[0], COST.get("", 3.0)) * 1e9),
            bytes_accessed=5 * 10**6,
            transcendentals=0,
        ),
    )(*args)
    return got[0] if single else list(got)


def total(refs):
    return sum(x[...].astype(F32) for x in refs)


def scale_of(v):
    return lax.rsqrt(jnp.mean(v * v, axis=-1, keepdims=True) + 1e-05)


def turned(d, r, n):
    return pl.ds(pl.multiple_of((d ^ r) * n, n & -n), n)


def pack_columns(w, k):
    rows = w.shape[0]
    c = w.shape[1] // (k * 16)

    def body(w_ref, o_ref):
        x = w_ref[...]
        for t in range(4):
            o_ref[t] = jnp.concatenate(
                [x[:, (i * 4 + t) * c : (i * 4 + t + 1) * c] for i in range(k * 4)], axis=1
            )

    return call(body, ((4, rows, k * 4 * c), w.dtype), w)


def lanes(n):
    return n - n % 128


def pair_up(gate, up):
    n = lanes(gate.shape[1])
    return jnp.concatenate([gate[:, :n], up[:, :n], gate[:, n:], up[:, n:]], axis=1)


def pair_down(x):
    half = x.shape[1] // 2
    n = lanes(half)
    gate = jnp.concatenate([x[:, :n], x[:, 2 * n : n + half]], axis=1)
    up = jnp.concatenate([x[:, n : 2 * n], x[:, n + half :]], axis=1)
    return gate, up


def pack_pairs(w):
    rows = w.shape[0]
    c = w.shape[1] // 32

    def body(w_ref, o_ref):
        x = w_ref[...]
        for t in range(4):
            sides = [
                jnp.concatenate(
                    [x[:, ((k * 4 + i) * 4 + t) * c : ((k * 4 + i) * 4 + t + 1) * c] for i in range(4)],
                    axis=1,
                )
                for k in range(2)
            ]
            o_ref[t] = pair_up(*sides)

    return call(body, ((4, rows, 8 * c), w.dtype), w)


def unpack_columns(blocks, k, scalars):
    rows = blocks[0].shape[0]
    c = blocks[0].shape[1] // (k * 4)

    def body(n_ref, *refs):
        o_ref, hold = refs[4], refs[5]
        for r in range(4):
            hold[n_ref[1] ^ r] = refs[r][...]
        x = [hold[t].astype(F32) for t in range(4)]
        if k == 2:
            x = [jnp.concatenate(pair_down(v), axis=1) for v in x]
        o_ref[...] = jnp.concatenate(
            [x[t][:, i * c : (i + 1) * c] for i in range(k * 4) for t in range(4)], axis=1
        )

    return call(
        body,
        ((rows, k * 16 * c), F32),
        *blocks,
        scalars=scalars,
        scratch=[((4, rows, 4 * k * c), blocks[0].dtype)],
    )


def pack_context(context, scalars):
    half = context.shape[0] // 2
    c = context.shape[1] // 16

    def body(n_ref, x_ref, *o_refs):
        s, t, d = n_ref[0], n_ref[1], n_ref[2]
        row = pl.multiple_of(s * half, half)
        for r in range(4):
            for q in range(4):
                col = pl.multiple_of(((d ^ q) * 4 + (t ^ r)) * c, c)
                o_refs[r][:, q * c : (q + 1) * c] = x_ref[pl.ds(row, half), pl.ds(col, c)]

    return call(body, [((half, 4 * c), context.dtype)] * 4, context, scalars=scalars)


def stack4(parts):
    n, c = parts[0].shape

    def body(*refs):
        for r in range(4):
            refs[4][r] = refs[r][...]

    return call(body, ((4, n, c), parts[0].dtype), *parts)


def unpack_context(own, other, scalars):
    half = own.shape[1]
    c = own.shape[2] // 4

    def body(n_ref, a_ref, b_ref, o_ref):
        s, t, d = n_ref[0], n_ref[1], n_ref[2]
        for ref, place in ((a_ref, s), (b_ref, 1 - s)):
            row = pl.multiple_of(place * half, half)
            for r in range(4):
                for q in range(4):
                    col = pl.multiple_of(((d ^ q) * 4 + (t ^ r)) * c, c)
                    o_ref[pl.ds(row, half), pl.ds(col, c)] = ref[
                        r, :, q * c : (q + 1) * c
                    ].astype(F32)

    return call(body, ((2 * half, 16 * c), F32), own, other, scalars=scalars)


def project(own, other, ins, some, scalars):
    half, feats = own.shape[1:]
    wide = ins[0].shape[0] - 16
    c = ins[0].shape[1]

    def body(n_ref, a_ref, b_ref, *refs):
        w_refs, g_ref, p_refs, w_all = refs[:4], refs[4], refs[5:9], refs[9]
        mine = pl.multiple_of(n_ref[0] * half, half)
        theirs = pl.multiple_of((1 - n_ref[0]) * half, half)
        for r in range(4):
            w_all[:, r * c : (r + 1) * c] = w_refs[r][:wide]
        gains = jnp.concatenate([w[wide:, :some] for w in w_refs], axis=1)
        for r in range(4):
            g_ref[pl.ds(r * 2 * half + mine, half)] = a_ref[r]
            g_ref[pl.ds(r * 2 * half + theirs, half)] = b_ref[r]
        x = mm(g_ref[...], w_all[...], NT).astype(BF)
        for r in range(4):
            p_refs[r][: 2 * half] = x[r * 2 * half : (r + 1) * 2 * half]
            p_refs[r][2 * half :] = gains

    outs = [((8 * half, feats), BF)] + [((2 * half + 16, wide), BF)] * 4
    got = call(body, outs, own, other, *ins, scalars=scalars, scratch=[((wide, feats), BF)])
    return got[0], got[1:]


def half_sum(parts):
    rows = parts[0].shape[0] - 16

    def body(a, b, c, e, o_ref):
        o_ref[...] = sum(x[:rows].astype(F32) for x in (a, b, c, e)).astype(BF)

    return call(body, ((rows, parts[0].shape[1]), BF), *parts)


def first_norm(own, other, parts, tokens, scalars):
    rows, wide = tokens.shape
    q = wide // 4
    some = parts[0].shape[1] // 4
    e = some // 2

    def body(n_ref, a_ref, b_ref, *refs):
        g_refs, t_ref, v_ref, n_out, gain_ref, hold = refs[:4], refs[4], refs[5], refs[6], refs[7], refs[8]
        s, t, d = n_ref[0], n_ref[1], n_ref[2]
        for r in range(4):
            hold[r * 8 : r * 8 + 8] = g_refs[r][rows : rows + 8].astype(F32)
        found = [hold[pl.ds(pl.multiple_of((t ^ j) * 8, 8), 8)][:1] for j in range(4)]
        for i in range(2):
            gain_ref[i : i + 1] = jnp.concatenate(
                [found[j][:, r * some + i * e : r * some + (i + 1) * e] for r in range(4) for j in range(4)],
                axis=1,
            )
        a = a_ref[...].astype(F32)
        b = b_ref[...].astype(F32)
        first = s == 0
        v = t_ref[...].astype(F32) + jnp.concatenate(
            [jnp.where(first, a, b), jnp.where(first, b, a)], axis=1
        )
        v_ref[...] = v
        scale = scale_of(v)
        for r in range(4):
            cols = slice(r * q, (r + 1) * q)
            n_out[:, cols] = (v_ref[:, turned(d, r, q)] * scale * gain_ref[0:1, cols]).astype(BF)

    return call(
        body,
        [((rows, wide), F32), ((rows, wide), BF), ((8, wide), F32)],
        own,
        other,
        *parts,
        tokens,
        scalars=scalars,
        scratch=[((32, 4 * some), F32)],
    )


def second_norm(start, parts, gains, scalars):
    rows, wide = start.shape
    q = wide // 4

    def body(n_ref, v_ref, a, b, c, e, gain_ref, m_ref, n_out):
        m = v_ref[...] + total((a, b, c, e))
        m_ref[...] = m
        scale = scale_of(m)
        for r in range(4):
            cols = slice(r * q, (r + 1) * q)
            n_out[:, cols] = (
                m_ref[:, turned(n_ref[2], r, q)] * scale * gain_ref[1:2, cols]
            ).astype(BF)

    return call(
        body,
        [((rows, wide), F32), ((rows, wide), BF)],
        start,
        *parts,
        gains,
        scalars=scalars,
    )


def norm_back(parts, value, gains, which, base, scalars, split):
    rows, wide = value.shape
    q = wide // 4

    def body(n_ref, a, b, c, e, v_ref, gain_ref, p_ref, o_ref, d_ref, *l_refs):
        s, d = n_ref[0], n_ref[2]
        grad = total((a, b, c, e))
        v = v_ref[...]
        scale = scale_of(v)
        inner = jnp.zeros((rows, 1), F32)
        for r in range(4):
            cols = slice(r * q, (r + 1) * q)
            unit = v_ref[:, turned(d, r, q)] * scale
            piece = grad[:, cols] * unit
            d_ref[0:1, turned(d, r, q)] = jnp.sum(piece, axis=0, keepdims=True)
            inner = inner + jnp.sum(piece * gain_ref[which : which + 1, cols], axis=-1, keepdims=True)
        inner = inner / wide
        for r in range(4):
            cols = slice(r * q, (r + 1) * q)
            at = turned(d, r, q)
            unit = v_ref[:, at] * scale
            o_ref[:, at] = p_ref[:, at].astype(F32) + scale * (
                grad[:, cols] * gain_ref[which : which + 1, cols] - unit * inner
            )
        if split:
            for ref, place in zip(l_refs, (s, 1 - s)):
                ref[...] = o_ref[:, pl.ds(pl.multiple_of(place * (wide // 2), wide // 2), wide // 2)].astype(BF)
        else:
            l_refs[0][...] = o_ref[...].astype(BF)

    low = [((rows, wide // 2), BF)] * 2 if split else [((rows, wide), BF)]
    return call(
        body,
        [((rows, wide), F32), ((8, wide), F32)] + low,
        *parts,
        value,
        gains,
        base,
        scalars=scalars,
    )


def beside(left, right):
    n, c = left.shape
    k, wide = right.shape

    def body(a_ref, b_ref, o_ref):
        o_ref[:, :c] = a_ref[...]
        for j in range(4):
            o_ref[j * k : (j + 1) * k, c:] = b_ref[:, j * (wide // 4) : (j + 1) * (wide // 4)]

    return call(body, ((n, c + wide // 4), left.dtype), left, right)


def query_key_value(chunks, ws):
    n, wide = chunks[0].shape
    k = ws[0].shape[0]
    c = k

    def body(*refs):
        c_refs, w_refs, q_ref, kv_ref, w_ref, all_ref = refs[:4], refs[4:8], refs[8], refs[9], refs[10], refs[11]
        for r in range(4):
            w_ref[r * k : (r + 1) * k] = w_refs[r][:, : 3 * c]
            all_ref[r * n : (r + 1) * n] = c_refs[r][...]
        x = mm(all_ref[...], w_ref[...]).astype(BF)
        q_ref[...] = x[:, :c]
        kv_ref[...] = x[:, c:]

    return call(
        body,
        [((4 * n, c), BF), ((4 * n, 2 * c), BF), ((4 * k, 3 * c), BF)],
        *chunks,
        *ws,
        scratch=[((4 * n, wide), BF)],
    )


def head_mask(c):
    i = lax.broadcasted_iota(jnp.int32, (c, c), 0) // HD
    j = lax.broadcasted_iota(jnp.int32, (c, c), 1) // HD
    return (i == j).astype(F32).astype(BF)


def head_sum(x, mask):
    high = x.astype(BF)
    low = (x - high.astype(F32)).astype(BF)
    return mm(high, mask) + mm(low, mask)


def attend(q, kv, far, ws, scalars):
    rows, c = q.shape
    n = rows // 4
    k, wide = c // 4, 4 * c

    def body(n_ref, q_ref, kv_ref, f_ref, *refs):
        o_refs, m_ref, w_ref, wo_ref, p_refs = refs[:4], refs[4], refs[5], refs[6], refs[7:]
        s, d = n_ref[0], n_ref[2]
        for r in range(4):
            for j in range(4):
                wo_ref[turned(d, r, k), j * c : (j + 1) * c] = o_refs[r][
                    j * k : (j + 1) * k, 3 * c :
                ]
        mask = head_mask(c)
        for r in range(4):
            at = slice(r * n, (r + 1) * n)
            own = kv_ref[at].astype(F32)
            other = f_ref[at].astype(F32)
            diff = head_sum(q_ref[at].astype(F32) * (own[:, :c] - other[:, :c]), mask)
            w = jnp.where(s == 0, 1.0, jax.nn.sigmoid(diff * HD ** (-0.5)))
            w_ref[at] = w
            mixed = (w * own[:, c:] + (1.0 - w) * other[:, c:]).astype(BF)
            m_ref[at] = mixed
        x = mm(m_ref[...], wo_ref[...]).astype(BF)
        for r in range(4):
            p_refs[r][...] = x[r * n : (r + 1) * n]

    return call(
        body,
        [((rows, c), BF), ((rows, c), F32), ((4 * k, wide), BF)] + [((n, wide), BF)] * 4,
        q,
        kv,
        far,
        *ws,
        scalars=scalars,
    )


def attend_back(chunks, wo, w, q, kv, far):
    n, wide = chunks[0].shape
    rows, c = q.shape

    def body(*refs):
        c_refs = refs[:4]
        wo_ref, w_ref, q_ref, kv_ref, f_ref, g_ref, b_ref, all_ref, gm_ref = refs[4:]
        mask = head_mask(c)
        for r in range(4):
            all_ref[r * n : (r + 1) * n] = c_refs[r][...]
        gm_ref[...] = mm(all_ref[...], wo_ref[...], NT)
        for r in range(4):
            at = slice(r * n, (r + 1) * n)
            gm = gm_ref[at]
            own = kv_ref[at].astype(F32)
            other = f_ref[at].astype(F32)
            w_own = w_ref[at]
            gs = (
                w_own
                * (1.0 - w_own)
                * head_sum(gm * (own[:, c:] - other[:, c:]), mask)
                * HD ** (-0.5)
            )
            gk = gs * q_ref[at].astype(F32)
            g_ref[at, :c] = gs * (own[:, :c] - other[:, :c])
            g_ref[at, c : 2 * c] = gk
            g_ref[at, 2 * c :] = w_own * gm
            b_ref[at, :c] = (-gk).astype(BF)
            b_ref[at, c:] = ((1.0 - w_own) * gm).astype(BF)

    return call(
        body,
        [((rows, 3 * c), F32), ((rows, 2 * c), BF)],
        *chunks,
        wo,
        w,
        q,
        kv,
        far,
        scratch=[((rows, wide), BF), ((rows, c), F32)],
    )


def into_normed(grad, back, w):
    rows, cols = grad.shape
    n, c = rows // 4, cols // 3

    def body(g_ref, b_ref, w_ref, l_ref, *p_refs):
        l_ref[:, :c] = g_ref[:, :c].astype(BF)
        l_ref[:, c:] = (g_ref[:, c:] + b_ref[...].astype(F32)).astype(BF)
        x = mm(l_ref[...], w_ref[...], NT).astype(BF)
        for r in range(4):
            p_refs[r][...] = x[r * n : (r + 1) * n]

    return call(
        body, [((rows, cols), BF)] + [((n, w.shape[0]), BF)] * 4, grad, back, w
    )


def parts_of(k, cols):
    return [((k, cols), BF), ((k, cols), BF), ((2 * k, cols), BF)]


def put_part(refs, r, value, cols=slice(None)):
    k = refs[0].shape[0]
    if r < 2:
        refs[r][:, cols] = value
    else:
        refs[2][(r - 2) * k : (r - 1) * k, cols] = value


def weight_parts(chunks, right):
    n, wide = chunks[0].shape
    q = wide // 4
    cols = right.shape[1]

    def body(*refs):
        c_refs, g_ref, o_refs, all_ref = refs[:4], refs[4], refs[5:8], refs[8]
        for r in range(4):
            all_ref[r * n : (r + 1) * n] = c_refs[r][...]
        for r in range(4):
            put_part(o_refs, r, mm(all_ref[:, r * q : (r + 1) * q], g_ref[...], TN).astype(BF))

    return call(body, parts_of(q, cols), *chunks, right, scratch=[((4 * n, wide), BF)])


def attention_parts(chunks, right, left, others, scalars):
    n, wide = chunks[0].shape
    q = wide // 4
    cols, c = right.shape[1], left.shape[1]
    k = c // 4

    def body(n_ref, *refs):
        c_refs, g_ref, l_ref, e_refs, o_refs, all_ref, x_ref = (
            refs[:4],
            refs[4],
            refs[5],
            refs[6:10],
            refs[10:13],
            refs[13],
            refs[14],
        )
        for r in range(4):
            all_ref[r * n : (r + 1) * n] = c_refs[r][...]
        for r in range(4):
            x = mm(all_ref[:, r * q : (r + 1) * q], g_ref[...], TN).astype(BF)
            put_part(o_refs, r, x, slice(0, cols))
        for r in range(4):
            all_ref[r * n : (r + 1) * n] = e_refs[r][...]
        x_ref[...] = mm(l_ref[...], all_ref[...], TN).astype(BF)
        for r in range(4):
            x = x_ref[turned(n_ref[2], r, k)]
            x = jnp.concatenate([x[:, j * c : (j + 1) * c] for j in range(4)], axis=0)
            put_part(o_refs, r, x, slice(cols, cols + c))

    return call(
        body,
        parts_of(q, cols + c),
        *chunks,
        right,
        left,
        *others,
        scalars=scalars,
        scratch=[((4 * n, wide), BF), ((c, wide), BF)],
    )


def row_parts(left, chunks, scalars):
    n, wide = chunks[0].shape
    k = left.shape[1]

    def body(n_ref, l_ref, *refs):
        c_refs, o_refs, all_ref, sum_ref = refs[:4], refs[4:7], refs[7], refs[8]
        for r in range(4):
            all_ref[r * n : (r + 1) * n] = c_refs[r][...]
        sum_ref[...] = mm(l_ref[...], all_ref[...], TN).astype(BF)
        for r in range(4):
            put_part(o_refs, r, sum_ref[turned(n_ref[2], r, k // 4)])

    return call(
        body,
        parts_of(k // 4, wide),
        left,
        *chunks,
        scalars=scalars,
        scratch=[((4 * n, wide), BF), ((k, wide), BF)],
    )


def for_far(pair, got):
    n = pair.shape[0] // 2

    def body(a_ref, b_ref, o_ref):
        o_ref[:n] = (a_ref[n:].astype(F32) + b_ref[:n].astype(F32)).astype(BF)
        o_ref[n:] = (a_ref[:n].astype(F32) + b_ref[n:].astype(F32)).astype(BF)

    return call(body, (pair.shape, BF), pair, got)


def for_near(near, got):
    n = near.shape[0]

    def body(a_ref, b_ref, o_ref):
        o_ref[...] = (a_ref[...].astype(F32) + b_ref[n:].astype(F32)).astype(BF)

    return call(body, (near.shape, BF), near, got)


def finished(own, near, far, dtype=F32):
    n = own.shape[0]

    def body(a_ref, b_ref, c_ref, o_ref):
        o_ref[...] = (
            a_ref[...].astype(F32) + b_ref[...].astype(F32) + c_ref[:n].astype(F32)
        ).astype(dtype)

    return call(body, (own.shape, dtype), own, near, far)


def finished_rows(own, near, far, scalars):
    n, cols = own.shape
    k = n // 4

    def body(n_ref, a_ref, b_ref, c_ref, *refs):
        refs[4][...] = (
            a_ref[...].astype(F32) + b_ref[...].astype(F32) + c_ref[:n].astype(F32)
        ).astype(BF)
        for r in range(4):
            refs[r][...] = refs[4][turned(n_ref[1], r, k)]

    return call(
        body,
        [((k, cols), BF)] * 4,
        own,
        near,
        far,
        scalars=scalars,
        scratch=[((n, cols), BF)],
    )


def finished_pair(own, near, far, scalars):
    n, cols = own.shape
    c = cols // 4
    k = n // 4

    def body(n_ref, a_ref, b_ref, c_ref, *refs):
        x = a_ref[...].astype(F32) + b_ref[...].astype(F32) + c_ref[:n].astype(F32)
        refs[5][...] = x[:, : 3 * c].astype(BF)
        for r in range(4):
            refs[r][...] = refs[5][turned(n_ref[1], r, k)]
        for j in range(4):
            refs[4][:, j * c : (j + 1) * c] = x[j * k : (j + 1) * k, 3 * c :]

    return call(
        body,
        [((k, 3 * c), BF)] * 4 + [((k, 4 * c), F32)],
        own,
        near,
        far,
        scalars=scalars,
        scratch=[((n, 3 * c), BF)],
    )


def finished_in(own, near, far):
    n = own.shape[0]
    k = n - 16

    def body(a_ref, b_ref, c_ref, o_ref, g_ref):
        o_ref[...] = (
            a_ref[:k].astype(F32) + b_ref[:k].astype(F32) + c_ref[:k].astype(F32)
        )
        g_ref[...] = (
            a_ref[k:].astype(F32) + b_ref[k:].astype(F32) + c_ref[k:n].astype(F32)
        )

    return call(body, [((k, own.shape[1]), F32), ((16, own.shape[1]), F32)], own, near, far)


def gate_and_up(chunks, ws):
    n, wide = chunks[0].shape
    cols = ws[0].shape[1]
    ff = cols // 2
    sizes = [x.shape[0] for x in ws]

    def body(*refs):
        c_refs, w_refs = refs[:4], refs[4 : 4 + len(ws)]
        w_ref, h_ref, a_ref, b_ref, all_ref, x_ref = refs[4 + len(ws) :]
        at = 0
        for ref, size in zip(w_refs, sizes):
            w_ref[at : at + size] = ref[...]
            at += size
        for r in range(4):
            all_ref[r * n : (r + 1) * n] = c_refs[r][...]
        x_ref[...] = mm(all_ref[...], w_ref[...])
        for r in range(4):
            rows = slice(r * n, (r + 1) * n)
            gate, up = pair_down(x_ref[rows])
            sig = jax.nn.sigmoid(gate)
            b = gate * sig
            h_ref[rows] = (b * up).astype(BF)
            a_ref[rows] = up * sig * (1.0 + gate * (1.0 - sig))
            b_ref[rows] = b

    return call(
        body,
        [((wide, cols), BF), ((4 * n, ff), BF), ((4 * n, ff), F32), ((4 * n, ff), F32)],
        *chunks,
        *ws,
        scratch=[((4 * n, wide), BF), ((4 * n, cols), F32)],
    )


def pick_chunks(cot, scalars):
    n, wide = cot.shape[1:]

    def body(n_ref, x_ref, *o_refs):
        for r in range(4):
            o_refs[r][...] = x_ref[n_ref[1] ^ r]

    return call(body, [((n, wide), BF)] * 4, cot, scalars=scalars)


def feed_back(chunks, downs, a, b, w, scalars):
    n, wide = chunks[0].shape
    k = downs[0].shape[0]
    ff = 4 * k

    def body(n_ref, *refs):
        c_refs, d_refs = refs[:4], refs[4:8]
        a_ref, b_ref, w_ref, dw_ref, g_ref = refs[8:13]
        p_refs, all_ref, x_ref = refs[13:17], refs[17], refs[18]
        for r in range(4):
            dw_ref[turned(n_ref[2], r, k)] = d_refs[r][...]
            all_ref[r * n : (r + 1) * n] = c_refs[r][...]
        x_ref[...] = mm(all_ref[...], dw_ref[...], NT)
        for r in range(4):
            rows = slice(r * n, (r + 1) * n)
            x = x_ref[rows]
            g_ref[rows] = pair_up(x * a_ref[rows], x * b_ref[rows]).astype(BF)
        all_ref[...] = mm(g_ref[...], w_ref[...], NT).astype(BF)
        for r in range(4):
            p_refs[r][...] = all_ref[r * n : (r + 1) * n]

    return call(
        body,
        [((ff, wide), BF), ((4 * n, 2 * ff), BF)] + [((n, wide), BF)] * 4,
        *chunks,
        *downs,
        a,
        b,
        w,
        scalars=scalars,
        scratch=[((4 * n, wide), BF), ((4 * n, ff), F32)],
    )


def down_parts(hidden, w):
    rows = hidden.shape[0]
    n = rows // 4

    def body(h_ref, w_ref, *p_refs):
        for r in range(4):
            p_refs[r][...] = mm(h_ref[r * n : (r + 1) * n], w_ref[...]).astype(BF)

    return call(body, [((n, w.shape[1]), BF)] * 4, hidden, w)


def proj_rows(keep, got, gain_one, gain_two):
    rows, c = keep.shape

    def body(a_ref, b_ref, g_ref, h_ref, o_ref):
        o_ref[:rows] = (a_ref[...].astype(F32) + b_ref[...].astype(F32)).astype(BF)
        gains = [x[0:1, i * c : (i + 1) * c] for x in (g_ref, h_ref) for i in range(2)]
        o_ref[rows:] = jnp.concatenate(gains + [jnp.zeros((12, c), F32)], axis=0).astype(BF)

    return call(body, ((rows + 16, c), BF), keep, got, gain_one, gain_two)


def context_terms(chunks, ins, scalars):
    n, wide = chunks[0].shape[0] - 16, chunks[0].shape[1]
    c = ins[0].shape[1]
    half = n // 2

    def body(n_ref, *refs):
        c_refs, w_refs, keep_ref, give_ref, w_all, x_ref, all_ref = (
            refs[:4],
            refs[4:8],
            refs[8],
            refs[9],
            refs[10],
            refs[11],
            refs[12],
        )
        mine = pl.multiple_of(n_ref[0] * half, half)
        theirs = pl.multiple_of((1 - n_ref[0]) * half, half)
        for r in range(4):
            w_all[:, r * c : (r + 1) * c] = w_refs[r][:wide]
            all_ref[r * n : (r + 1) * n] = c_refs[r][:n]
        x_ref[...] = mm(all_ref[...], w_all[...]).astype(BF)
        for r in range(4):
            keep_ref[r] = x_ref[pl.ds(r * n + mine, half)]
            give_ref[r] = x_ref[pl.ds(r * n + theirs, half)]

    return call(
        body,
        [((4, half, 4 * c), BF)] * 2,
        *chunks,
        *ins,
        scalars=scalars,
        scratch=[((wide, 4 * c), BF), ((4 * n, 4 * c), BF), ((4 * n, wide), BF)],
    )


def both_terms(keep, got):
    half, feats = keep.shape[1:]

    def body(a_ref, b_ref, *o_refs):
        for r in range(4):
            o_refs[r][...] = (a_ref[r].astype(F32) + b_ref[r].astype(F32)).astype(BF)

    return call(body, [((half, feats), BF)] * 4, keep, got)


def in_parts(chunks, group, scalars):
    n, wide = chunks[0].shape[0] - 16, chunks[0].shape[1]
    c = group.shape[1] // 4

    def body(n_ref, *refs):
        c_refs, g_ref, o_refs, all_ref, hold = refs[:4], refs[4], refs[5:8], refs[8], refs[9]
        for r in range(4):
            all_ref[r * n : (r + 1) * n] = c_refs[r][:n]
        gains = sum(x[n:].astype(F32) for x in c_refs)
        for i in range(4):
            for k in range(2):
                row = gains[2 * k + i // 2 : 2 * k + i // 2 + 1, (i % 2) * c : (i % 2 + 1) * c]
                hold[i, k : k + 1] = row
            hold[i, 2:] = jnp.zeros((14, c), F32)
        x = mm(all_ref[...], g_ref[...], TN).astype(BF)
        for r in range(4):
            below = hold[n_ref[2] ^ r].astype(BF)
            put_part(
                o_refs, r, jnp.concatenate([x[:, r * c : (r + 1) * c], below], axis=0)
            )

    return call(
        body,
        parts_of(wide + 16, c),
        *chunks,
        group,
        scalars=scalars,
        scratch=[((4 * n, wide), BF), ((4, 16, c), F32)],
    )


def add(*parts, dtype=F32):
    def body(*refs):
        refs[-1][...] = total(refs[:-1]).astype(dtype)

    return call(body, (parts[0].shape, dtype), *parts)


def on_device(
    tokens, context, w_in, attn_gain, w_qkv, w_out, ffn_gain, w_gate_up, w_down, cotangent
):
    s = lax.axis_index("stream")
    t = lax.axis_index("t")
    d = lax.axis_index("d1")
    many = lax.axis_size("d2") > 1
    frames = tokens.shape[0]
    wide = tokens.shape[2]
    scalars = jnp.stack([s, t, d]).astype(jnp.int32)

    def near(w, axis=0):
        return lax.all_gather(w, "d2", axis=axis, tiled=True) if many else w

    def near_sum(g, axis=0):
        return lax.psum_scatter(g, "d2", scatter_dimension=axis, tiled=True) if many else g

    tokens = tokens[:, 0]
    cotangent = cotangent[:, 0]

    gains = jnp.concatenate([near(attn_gain[0]), near(ffn_gain[0])])
    some = gains.shape[0]
    in_mine = near(w_in, 1)
    in_mine = jnp.concatenate(
        [in_mine, jnp.pad(gains[None], ((0, 15), (0, in_mine.shape[1] - some)))]
    )
    fly = Flying()
    in_one, in_three = zhop(in_mine, 1), zhop(in_mine, 3)
    parts = pack_context(context, scalars)
    got = {r: hop(parts[r], r) for r in (3, 2, 1)}
    packed = pack_columns(tie(near(w_qkv[0]), parts[0]), 3)
    if 26 in SKIP:
        packed = tie(packed, in_three)
    qkv_mine = lax.all_to_all(packed, "t", 0, 0, tiled=True).reshape(-1, packed.shape[2])
    packed = pack_pairs(tie(near(w_gate_up[0]), qkv_mine))
    gu_mine = lax.all_to_all(packed, "t", 0, 0, tiled=True).reshape(-1, packed.shape[2])
    fly["gu"] = gu_mine
    own = tie(stack4([parts[0], got[1], got[2], got[3]]), qkv_mine)
    other = swap(own)
    in_two = zhop(opt(0, in_three, own), 1)
    ins = [in_mine, in_one, in_two, in_three]
    qkv_mine = beside(qkv_mine, near(w_out[0]))
    fly["qkv1"], fly["qkv3"] = zhop(qkv_mine, 1), zhop(qkv_mine, 3)
    group, parts = project(own, fly.due("group", other), ins, some, scalars)

    parts[0] = fly.due("parts0", parts[0])
    parts = collect(parts)
    proj_half = fly.due("half", half_sum(parts))
    start, mine, gains = first_norm(proj_half, swap(proj_half), parts, tokens, scalars)
    mine = fly.due("mine1", mine)
    by_x, by_y = hop(mine, 1), hop(mine, 2)
    fly["qkv2"] = zhop(opt(1, fly["qkv3"], mine), 1)
    by_y = fly.due("byy1", by_y)
    by_xy = corner(30, by_y, mine)
    gu_mine = opt(2, gu_mine, by_y)
    upper, lower = gu_mine[: gu_mine.shape[0] // 2], gu_mine[gu_mine.shape[0] // 2 :]
    whole = 37 in SKIP
    fly["gu1"], fly["up3"] = zhop(gu_mine, 1), zhop(gu_mine if whole else upper, 3)
    ws = [qkv_mine, fly["qkv1"], fly["qkv2"], fly["qkv3"]]
    chunks_one = [mine, by_x, by_y, fly.due("byxy1", by_xy)]
    q, kv, qkv_w = query_key_value(chunks_one, ws)
    if 36 in SKIP:
        cot = opt(3, cotangent, q)
        fly["coty"], fly["cotx"] = hop(cot, 2), hop(cot, 1)
    else:
        fly["cot"] = lax.all_to_all(
            jnp.broadcast_to(opt(3, cotangent, q)[None], (4, frames, wide)), "t", 0, 0, tiled=True
        )
    far = lax.ppermute(fly.due("kv", kv), "stream", [(0, 1)])
    if not whole:
        fly["low3"] = zhop(opt(4, lower, q), 3)
    mixed, w_own, out_w, *parts = attend(q, kv, far, ws, scalars)
    fly["up2"] = zhop(opt(5, fly["up3"], mixed), 1)
    parts[0] = fly.due("parts1", parts[0])
    parts = collect(parts)
    parts[0] = fly.due("mid", parts[0])
    middle, mine = second_norm(start, parts, gains, scalars)
    if not whole:
        fly["low2"] = zhop(opt(6, fly["low3"], middle), 1)
    if 36 in SKIP:
        fly["cotxy"] = corner(38, opt(39, fly["coty"], middle), cot)
    down_mine = near(w_down[0])
    fly["down1"] = zhop(opt(7, down_mine, middle), 1)

    mine = fly.due("mine2", mine)
    by_x, by_y = hop(mine, 1), hop(mine, 2)
    by_y = fly.due("byy2", by_y)
    by_xy = corner(31, by_y, mine)
    fly["down3"] = zhop(opt(8, down_mine, mine), 3)
    chunks_two = [mine, by_x, by_y, fly.due("byxy2", by_xy)]
    gus = [gu_mine, fly["gu1"], fly["up2"], fly["up3"]]
    if not whole:
        gus = [gu_mine, fly["gu1"], fly["up2"], fly["low2"], fly["up3"], fly["low3"]]
    gu_w, hidden, a, b = gate_and_up(chunks_two, gus)
    fly["down2"] = zhop(opt(9, fly["down3"], by_xy), 1)
    hidden = fly.due("hidden", hidden)
    if 36 in SKIP:
        cot = [cot, fly["cotx"], fly["coty"], fly["cotxy"]]
    else:
        cot = pick_chunks(fly["cot"].reshape(4, frames, wide), scalars)
    g = row_parts(hidden, cot, scalars)
    far_g = inward(opt(10, g[2], fly["down2"]))
    fly["g1"] = far_g
    downs = [down_mine, fly["down1"], fly["down2"], fly["down3"]]
    down_w, grad_gu, *parts = feed_back([opt(11, cot[0], g[0])] + cot[1:], downs, a, b, gu_w, scalars)
    u = weight_parts(chunks_two, opt(12, grad_gu, parts[0]))
    far_u = inward(u[2])
    fly["u1"] = far_u
    parts[0] = fly.due("parts2", parts[0])
    parts = collect(parts)
    parts[0] = fly.due("nb2", parts[0])
    far_g = across(for_far(g[2], opt(13, far_g, parts[0])))
    fly["g2"] = far_g
    grad_middle, gain_two, mine = norm_back(
        parts, middle, gains, 1, cotangent, scalars, False
    )
    mine = fly.due("mine3", mine)
    branch = [mine, hop(mine, 1), hop(mine, 2)]
    branch[2] = fly.due("byy3", branch[2])
    branch.append(fly.due("branch", corner(32, branch[2], mine)))
    near_g = zhop(for_near(g[1], opt(14, far_g, branch[3])), 1)
    fly["g3"] = near_g

    grad, back = attend_back(branch, out_w, w_own, q, kv, far)
    back = lax.ppermute(fly.due("back", back), "stream", [(1, 0)])
    parts = collect(down_parts(opt(15, hidden, branch[3]), down_w))
    result = add(middle, *parts)
    fly["result"] = result
    far_u = across(for_far(u[2], opt(16, far_u, back)))
    fly["u2"] = far_u
    grad_qkv, *parts = into_normed(grad, fly.due("into", back), qkv_w)
    parts[0] = fly.due("parts3", parts[0])
    h = attention_parts(chunks_one, opt(17, grad_qkv, parts[0]), mixed, branch, scalars)
    far_h = inward(h[2])
    fly["h1"] = far_h
    parts = collect(parts)
    parts[0] = fly.due("nb1", parts[0])
    grad_start, gain_one, keep, give = norm_back(
        parts, start, gains, 0, grad_middle, scalars, True
    )
    grad_proj = proj_rows(fly.due("keep", keep), swap(give), gain_one, gain_two)
    far_h = across(for_far(h[2], opt(18, far_h, grad_proj)))
    fly["h2"] = far_h
    gproj = [grad_proj, hop(grad_proj, 1), hop(grad_proj, 2)]
    gproj[2] = fly.due("gpy", gproj[2])
    gproj.append(fly.due("gproj", corner(33, gproj[2], grad_proj)))
    near_u = zhop(for_near(u[1], opt(19, far_u, gproj[3])), 1)
    fly["u3"] = near_u

    g_in = in_parts(gproj, group, scalars)
    far_in = inward(g_in[2])
    fly["in1"] = far_in
    keep, give = context_terms([opt(20, gproj[0], g_in[0])] + gproj[1:], ins, scalars)
    both = both_terms(keep, fly.due("both", swap(fly.due("give", give))))
    got = [both[0]] + [hop(both[r], r) for r in (1, 2, 3)]
    got = fly.due("got", stack4(got))
    blocks = finished_rows(u[0], near_u, opt(21, far_u, got), scalars)
    g_gu = [blocks[0]] + [hop(blocks[r], r) for r in (1, 2, 3)]
    far_in = across(for_far(g_in[2], opt(22, far_in, got)))
    fly["in2"] = far_in
    near_h = zhop(for_near(h[1], opt(23, far_h, got)), 1)
    fly["h3"] = near_h
    other = swap(got)
    g_gu[0] = fly.due("gu_out", g_gu[0])
    grad_gate_up = unpack_columns(g_gu, 2, scalars)
    near_in = zhop(for_near(g_in[1], opt(24, far_in, grad_gate_up)), 1)
    fly["in3"] = near_in
    *blocks, grad_out = finished_pair(h[0], near_h, opt(25, far_h, grad_gate_up), scalars)
    g_qkv = [blocks[0]] + [hop(blocks[r], r) for r in (1, 2, 3)]
    grad_context = unpack_context(got, fly.due("context", other), scalars)
    grad_gate_up = near_sum(grad_gate_up)
    grad_qkv = near_sum(unpack_columns(g_qkv, 3, scalars))
    grad_out = near_sum(grad_out)
    grad_down = near_sum(finished(g[0], near_g, fly["g2"]))
    grad_in, found = finished_in(g_in[0], near_in, far_in)
    grad_in = near_sum(grad_in, 1)
    found = lax.dynamic_slice_in_dim(found[:2], t * (some // 2), some // 2, 1)
    gains = near_sum(found, 1)
    return (
        result[:, None],
        grad_start[:, None],
        grad_context,
        grad_in,
        gains[:1],
        grad_qkv[None],
        grad_out[None],
        gains[1:],
        grad_gate_up[None],
        grad_down[None],
    )


def solution(mesh):
    n = mesh.shape["frames"]
    grid = Mesh(mesh.devices.reshape(2, 4, 4, n // 16), ("stream", "d1", "t", "d2"))
    f = ("d1", "t", "d2")
    return jax.shard_map(
        on_device,
        mesh=grid,
        in_specs=(
            P(f, "stream", None),
            P(f, None),
            P("stream", f),
            P("stream", f),
            P("stream", f, None),
            P("stream", f, None),
            P("stream", f),
            P("stream", f, None),
            P("stream", f, None),
            P(f, "stream", None),
        ),
        out_specs=(
            P(f, "stream", None),
            P(f, "stream", None),
            P(f, None),
            P("stream", f),
            P("stream", f),
            P("stream", f, None),
            P("stream", f, None),
            P("stream", f),
            P("stream", f, None),
            P("stream", f, None),
        ),
        check_vma=False,
    )
```

```python
import jax
import jax.numpy as jnp
from jax import lax
from jax.experimental import pallas as pl
from jax.experimental.pallas import tpu as pltpu
from jax.sharding import Mesh
from jax.sharding import PartitionSpec as P

HD = 64
F32 = jnp.float32
BF = jnp.bfloat16
NN = (((1,), (0,)), ((), ()))
NT = (((1,), (1,)), ((), ()))
TN = (((0,), (0,)), ((), ()))


def mm(a, b, form=NN):
    return lax.dot_general(a, b, form, preferred_element_type=F32)


DUE = {
    "gu": "half",
    "qkv3": "half",
    "qkv1": "mine1",
    "qkv2": "byy1",
    "up3": "kv",
    "gu1": "byxy1",
    "cot": "mid",
    "low3": "mid",
    "up2": "byy2",
    "down1": "mine2",
    "g1": "nb2",
    "g2": "branch",
    "u1": "nb1",
    "result": "into",
    "h1": "gpy",
    "u2": "give",
    "in1": "context",
    "u3": "both",
    "h2": "got",
    "h3": "gu_out",
    "in2": "gu_out",
    "down3": "hidden",
    "g3": "context",
}
SKIP = (6, 7, 14, 20, 23, 32, 33, 36)
COST = {
    "": 3.0,
    "unpack_columns": 10.0,
    "row_parts": 10.0,
    "pack_pairs": 0.3,
    "stack4": 1.0,
}


def tie(x, *after):
    return lax.optimization_barrier((x,) + after)[0]


def opt(i, x, *after):
    return x if i in SKIP else tie(x, *after)


def corner(i, by_y, x):
    return hop(by_y, 1) if i not in SKIP else hop(x, 3)


class Flying(dict):
    def due(self, point, x):
        after = [v for k, v in self.items() if DUE.get(k) == point]
        return tie(x, *after) if after else x


def hop(x, r):
    return lax.ppermute(x, "t", [(i, i ^ r) for i in range(4)])


def zhop(x, r):
    return lax.ppermute(x, "d1", [(i, i ^ r) for i in range(4)])


def inward(x):
    return lax.ppermute(x, "d1", [(0, 1), (3, 2)])


def across(x):
    return lax.ppermute(x, "d1", [(1, 2), (2, 1)])


def swap(x):
    return lax.ppermute(x, "stream", [(0, 1), (1, 0)])


def collect(parts):
    return [parts[0]] + [hop(parts[r], r) for r in (1, 2, 3)]


def call(body, outs, *args, scalars=None, scratch=()):
    inside = [pl.BlockSpec(memory_space=pltpu.VMEM)] * len(args)
    if scalars is not None:
        inside = [pl.BlockSpec(memory_space=pltpu.SMEM)] + inside
        args = (scalars,) + args
    single = not isinstance(outs, list)
    shapes = [jax.ShapeDtypeStruct(*o) for o in ([outs] if single else outs)]
    got = pl.pallas_call(
        body,
        out_shape=shapes,
        in_specs=inside,
        out_specs=[pl.BlockSpec(memory_space=pltpu.VMEM)] * len(shapes),
        scratch_shapes=[pltpu.VMEM(*x) for x in scratch],
        compiler_params=pltpu.CompilerParams(vmem_limit_bytes=24 << 20),
        cost_estimate=pl.CostEstimate(
            flops=int(COST.get(body.__qualname__.split(".")[0], COST.get("", 3.0)) * 1e9),
            bytes_accessed=5 * 10**6,
            transcendentals=0,
        ),
    )(*args)
    return got[0] if single else list(got)


def total(refs):
    return sum(x[...].astype(F32) for x in refs)


def scale_of(v):
    return lax.rsqrt(jnp.mean(v * v, axis=-1, keepdims=True) + 1e-05)


def turned(d, r, n):
    return pl.ds(pl.multiple_of((d ^ r) * n, n & -n), n)


def pack_columns(w, k):
    rows = w.shape[0]
    c = w.shape[1] // (k * 16)

    def body(w_ref, o_ref):
        x = w_ref[...]
        for t in range(4):
            o_ref[t] = jnp.concatenate(
                [x[:, (i * 4 + t) * c : (i * 4 + t + 1) * c] for i in range(k * 4)], axis=1
            )

    return call(body, ((4, rows, k * 4 * c), w.dtype), w)


def lanes(n):
    return n - n % 128


def pair_up(gate, up):
    n = lanes(gate.shape[1])
    return jnp.concatenate([gate[:, :n], up[:, :n], gate[:, n:], up[:, n:]], axis=1)


def pair_down(x):
    half = x.shape[1] // 2
    n = lanes(half)
    gate = jnp.concatenate([x[:, :n], x[:, 2 * n : n + half]], axis=1)
    up = jnp.concatenate([x[:, n : 2 * n], x[:, n + half :]], axis=1)
    return gate, up


def pack_pairs(w):
    rows = w.shape[0]
    c = w.shape[1] // 32

    def body(w_ref, o_ref):
        x = w_ref[...]
        for t in range(4):
            sides = [
                jnp.concatenate(
                    [x[:, ((k * 4 + i) * 4 + t) * c : ((k * 4 + i) * 4 + t + 1) * c] for i in range(4)],
                    axis=1,
                )
                for k in range(2)
            ]
            o_ref[t] = pair_up(*sides)

    return call(body, ((4, rows, 8 * c), w.dtype), w)


def unpack_columns(blocks, k, scalars):
    rows = blocks[0].shape[0]
    c = blocks[0].shape[1] // (k * 4)

    def body(n_ref, *refs):
        o_ref, hold = refs[4], refs[5]
        for r in range(4):
            hold[n_ref[1] ^ r] = refs[r][...]
        x = [hold[t].astype(F32) for t in range(4)]
        if k == 2:
            x = [jnp.concatenate(pair_down(v), axis=1) for v in x]
        o_ref[...] = jnp.concatenate(
            [x[t][:, i * c : (i + 1) * c] for i in range(k * 4) for t in range(4)], axis=1
        )

    return call(
        body,
        ((rows, k * 16 * c), F32),
        *blocks,
        scalars=scalars,
        scratch=[((4, rows, 4 * k * c), blocks[0].dtype)],
    )


def pack_context(context, scalars):
    half = context.shape[0] // 2
    c = context.shape[1] // 16

    def body(n_ref, x_ref, *o_refs):
        s, t, d = n_ref[0], n_ref[1], n_ref[2]
        row = pl.multiple_of(s * half, half)
        for r in range(4):
            for q in range(4):
                col = pl.multiple_of(((d ^ q) * 4 + (t ^ r)) * c, c)
                o_refs[r][:, q * c : (q + 1) * c] = x_ref[pl.ds(row, half), pl.ds(col, c)]

    return call(body, [((half, 4 * c), context.dtype)] * 4, context, scalars=scalars)


def stack4(parts):
    n, c = parts[0].shape

    def body(*refs):
        for r in range(4):
            refs[4][r] = refs[r][...]

    return call(body, ((4, n, c), parts[0].dtype), *parts)


def unpack_context(own, other, scalars):
    half = own.shape[1]
    c = own.shape[2] // 4

    def body(n_ref, a_ref, b_ref, o_ref):
        s, t, d = n_ref[0], n_ref[1], n_ref[2]
        for ref, place in ((a_ref, s), (b_ref, 1 - s)):
            row = pl.multiple_of(place * half, half)
            for r in range(4):
                for q in range(4):
                    col = pl.multiple_of(((d ^ q) * 4 + (t ^ r)) * c, c)
                    o_ref[pl.ds(row, half), pl.ds(col, c)] = ref[
                        r, :, q * c : (q + 1) * c
                    ].astype(F32)

    return call(body, ((2 * half, 16 * c), F32), own, other, scalars=scalars)


def project(own, other, ins, some, scalars):
    half, feats = own.shape[1:]
    wide = ins[0].shape[0] - 16
    c = ins[0].shape[1]

    def body(n_ref, a_ref, b_ref, *refs):
        w_refs, g_ref, p_refs, w_all = refs[:4], refs[4], refs[5:9], refs[9]
        mine = pl.multiple_of(n_ref[0] * half, half)
        theirs = pl.multiple_of((1 - n_ref[0]) * half, half)
        for r in range(4):
            w_all[:, r * c : (r + 1) * c] = w_refs[r][:wide]
        gains = jnp.concatenate([w[wide:, :some] for w in w_refs], axis=1)
        for r in range(4):
            g_ref[pl.ds(r * 2 * half + mine, half)] = a_ref[r]
            g_ref[pl.ds(r * 2 * half + theirs, half)] = b_ref[r]
        x = mm(g_ref[...], w_all[...], NT).astype(BF)
        for r in range(4):
            p_refs[r][: 2 * half] = x[r * 2 * half : (r + 1) * 2 * half]
            p_refs[r][2 * half :] = gains

    outs = [((8 * half, feats), BF)] + [((2 * half + 16, wide), BF)] * 4
    got = call(body, outs, own, other, *ins, scalars=scalars, scratch=[((wide, feats), BF)])
    return got[0], got[1:]


def half_sum(parts):
    rows = parts[0].shape[0] - 16

    def body(a, b, c, e, o_ref):
        o_ref[...] = sum(x[:rows].astype(F32) for x in (a, b, c, e)).astype(BF)

    return call(body, ((rows, parts[0].shape[1]), BF), *parts)


def first_norm(own, other, parts, tokens, scalars):
    rows, wide = tokens.shape
    q = wide // 4
    some = parts[0].shape[1] // 4
    e = some // 2

    def body(n_ref, a_ref, b_ref, *refs):
        g_refs, t_ref, v_ref, n_out, gain_ref, hold = refs[:4], refs[4], refs[5], refs[6], refs[7], refs[8]
        s, t, d = n_ref[0], n_ref[1], n_ref[2]
        for r in range(4):
            hold[r * 8 : r * 8 + 8] = g_refs[r][rows : rows + 8].astype(F32)
        found = [hold[pl.ds(pl.multiple_of((t ^ j) * 8, 8), 8)][:1] for j in range(4)]
        for i in range(2):
            gain_ref[i : i + 1] = jnp.concatenate(
                [found[j][:, r * some + i * e : r * some + (i + 1) * e] for r in range(4) for j in range(4)],
                axis=1,
            )
        a = a_ref[...].astype(F32)
        b = b_ref[...].astype(F32)
        first = s == 0
        v = t_ref[...].astype(F32) + jnp.concatenate(
            [jnp.where(first, a, b), jnp.where(first, b, a)], axis=1
        )
        v_ref[...] = v
        scale = scale_of(v)
        for r in range(4):
            cols = slice(r * q, (r + 1) * q)
            n_out[:, cols] = (v_ref[:, turned(d, r, q)] * scale * gain_ref[0:1, cols]).astype(BF)

    return call(
        body,
        [((rows, wide), F32), ((rows, wide), BF), ((8, wide), F32)],
        own,
        other,
        *parts,
        tokens,
        scalars=scalars,
        scratch=[((32, 4 * some), F32)],
    )


def second_norm(start, parts, gains, scalars):
    rows, wide = start.shape
    q = wide // 4

    def body(n_ref, v_ref, a, b, c, e, gain_ref, m_ref, n_out):
        m = v_ref[...] + total((a, b, c, e))
        m_ref[...] = m
        scale = scale_of(m)
        for r in range(4):
            cols = slice(r * q, (r + 1) * q)
            n_out[:, cols] = (
                m_ref[:, turned(n_ref[2], r, q)] * scale * gain_ref[1:2, cols]
            ).astype(BF)

    return call(
        body,
        [((rows, wide), F32), ((rows, wide), BF)],
        start,
        *parts,
        gains,
        scalars=scalars,
    )


def norm_back(parts, value, gains, which, base, scalars, split):
    rows, wide = value.shape
    q = wide // 4

    def body(n_ref, a, b, c, e, v_ref, gain_ref, p_ref, o_ref, d_ref, *l_refs):
        s, d = n_ref[0], n_ref[2]
        grad = total((a, b, c, e))
        v = v_ref[...]
        scale = scale_of(v)
        inner = jnp.zeros((rows, 1), F32)
        for r in range(4):
            cols = slice(r * q, (r + 1) * q)
            unit = v_ref[:, turned(d, r, q)] * scale
            piece = grad[:, cols] * unit
            d_ref[0:1, turned(d, r, q)] = jnp.sum(piece, axis=0, keepdims=True)
            inner = inner + jnp.sum(piece * gain_ref[which : which + 1, cols], axis=-1, keepdims=True)
        inner = inner / wide
        for r in range(4):
            cols = slice(r * q, (r + 1) * q)
            at = turned(d, r, q)
            unit = v_ref[:, at] * scale
            o_ref[:, at] = p_ref[:, at].astype(F32) + scale * (
                grad[:, cols] * gain_ref[which : which + 1, cols] - unit * inner
            )
        if split:
            for ref, place in zip(l_refs, (s, 1 - s)):
                ref[...] = o_ref[:, pl.ds(pl.multiple_of(place * (wide // 2), wide // 2), wide // 2)].astype(BF)
        else:
            l_refs[0][...] = o_ref[...].astype(BF)

    low = [((rows, wide // 2), BF)] * 2 if split else [((rows, wide), BF)]
    return call(
        body,
        [((rows, wide), F32), ((8, wide), F32)] + low,
        *parts,
        value,
        gains,
        base,
        scalars=scalars,
    )


def beside(left, right):
    n, c = left.shape
    k, wide = right.shape

    def body(a_ref, b_ref, o_ref):
        o_ref[:, :c] = a_ref[...]
        for j in range(4):
            o_ref[j * k : (j + 1) * k, c:] = b_ref[:, j * (wide // 4) : (j + 1) * (wide // 4)]

    return call(body, ((n, c + wide // 4), left.dtype), left, right)


def query_key_value(chunks, ws):
    n, wide = chunks[0].shape
    k = ws[0].shape[0]
    c = k

    def body(*refs):
        c_refs, w_refs, q_ref, kv_ref, w_ref, all_ref = refs[:4], refs[4:8], refs[8], refs[9], refs[10], refs[11]
        for r in range(4):
            w_ref[r * k : (r + 1) * k] = w_refs[r][:, : 3 * c]
            all_ref[r * n : (r + 1) * n] = c_refs[r][...]
        x = mm(all_ref[...], w_ref[...]).astype(BF)
        q_ref[...] = x[:, :c]
        kv_ref[...] = x[:, c:]

    return call(
        body,
        [((4 * n, c), BF), ((4 * n, 2 * c), BF), ((4 * k, 3 * c), BF)],
        *chunks,
        *ws,
        scratch=[((4 * n, wide), BF)],
    )


def head_mask(c):
    i = lax.broadcasted_iota(jnp.int32, (c, c), 0) // HD
    j = lax.broadcasted_iota(jnp.int32, (c, c), 1) // HD
    return (i == j).astype(F32).astype(BF)


def head_sum(x, mask):
    high = x.astype(BF)
    low = (x - high.astype(F32)).astype(BF)
    return mm(high, mask) + mm(low, mask)


def attend(q, kv, far, ws, scalars):
    rows, c = q.shape
    n = rows // 4
    k, wide = c // 4, 4 * c

    def body(n_ref, q_ref, kv_ref, f_ref, *refs):
        o_refs, m_ref, w_ref, wo_ref, p_refs = refs[:4], refs[4], refs[5], refs[6], refs[7:]
        s, d = n_ref[0], n_ref[2]
        for r in range(4):
            for j in range(4):
                wo_ref[turned(d, r, k), j * c : (j + 1) * c] = o_refs[r][
                    j * k : (j + 1) * k, 3 * c :
                ]
        mask = head_mask(c)
        for r in range(4):
            at = slice(r * n, (r + 1) * n)
            own = kv_ref[at].astype(F32)
            other = f_ref[at].astype(F32)
            diff = head_sum(q_ref[at].astype(F32) * (own[:, :c] - other[:, :c]), mask)
            w = jnp.where(s == 0, 1.0, jax.nn.sigmoid(diff * HD ** (-0.5)))
            w_ref[at] = w
            mixed = (w * own[:, c:] + (1.0 - w) * other[:, c:]).astype(BF)
            m_ref[at] = mixed
        x = mm(m_ref[...], wo_ref[...]).astype(BF)
        for r in range(4):
            p_refs[r][...] = x[r * n : (r + 1) * n]

    return call(
        body,
        [((rows, c), BF), ((rows, c), F32), ((4 * k, wide), BF)] + [((n, wide), BF)] * 4,
        q,
        kv,
        far,
        *ws,
        scalars=scalars,
    )


def attend_back(chunks, wo, w, q, kv, far):
    n, wide = chunks[0].shape
    rows, c = q.shape

    def body(*refs):
        c_refs = refs[:4]
        wo_ref, w_ref, q_ref, kv_ref, f_ref, g_ref, b_ref, all_ref, gm_ref = refs[4:]
        mask = head_mask(c)
        for r in range(4):
            all_ref[r * n : (r + 1) * n] = c_refs[r][...]
        gm_ref[...] = mm(all_ref[...], wo_ref[...], NT)
        for r in range(4):
            at = slice(r * n, (r + 1) * n)
            gm = gm_ref[at]
            own = kv_ref[at].astype(F32)
            other = f_ref[at].astype(F32)
            w_own = w_ref[at]
            gs = (
                w_own
                * (1.0 - w_own)
                * head_sum(gm * (own[:, c:] - other[:, c:]), mask)
                * HD ** (-0.5)
            )
            gk = gs * q_ref[at].astype(F32)
            g_ref[at, :c] = gs * (own[:, :c] - other[:, :c])
            g_ref[at, c : 2 * c] = gk
            g_ref[at, 2 * c :] = w_own * gm
            b_ref[at, :c] = (-gk).astype(BF)
            b_ref[at, c:] = ((1.0 - w_own) * gm).astype(BF)

    return call(
        body,
        [((rows, 3 * c), F32), ((rows, 2 * c), BF)],
        *chunks,
        wo,
        w,
        q,
        kv,
        far,
        scratch=[((rows, wide), BF), ((rows, c), F32)],
    )


def into_normed(grad, back, w):
    rows, cols = grad.shape
    n, c = rows // 4, cols // 3

    def body(g_ref, b_ref, w_ref, l_ref, *p_refs):
        l_ref[:, :c] = g_ref[:, :c].astype(BF)
        l_ref[:, c:] = (g_ref[:, c:] + b_ref[...].astype(F32)).astype(BF)
        x = mm(l_ref[...], w_ref[...], NT).astype(BF)
        for r in range(4):
            p_refs[r][...] = x[r * n : (r + 1) * n]

    return call(
        body, [((rows, cols), BF)] + [((n, w.shape[0]), BF)] * 4, grad, back, w
    )


def parts_of(k, cols):
    return [((k, cols), BF), ((k, cols), BF), ((2 * k, cols), BF)]


def put_part(refs, r, value, cols=slice(None)):
    k = refs[0].shape[0]
    if r < 2:
        refs[r][:, cols] = value
    else:
        refs[2][(r - 2) * k : (r - 1) * k, cols] = value


def weight_parts(chunks, right):
    n, wide = chunks[0].shape
    q = wide // 4
    cols = right.shape[1]

    def body(*refs):
        c_refs, g_ref, o_refs, all_ref = refs[:4], refs[4], refs[5:8], refs[8]
        for r in range(4):
            all_ref[r * n : (r + 1) * n] = c_refs[r][...]
        for r in range(4):
            put_part(o_refs, r, mm(all_ref[:, r * q : (r + 1) * q], g_ref[...], TN).astype(BF))

    return call(body, parts_of(q, cols), *chunks, right, scratch=[((4 * n, wide), BF)])


def attention_parts(chunks, right, left, others, scalars):
    n, wide = chunks[0].shape
    q = wide // 4
    cols, c = right.shape[1], left.shape[1]
    k = c // 4

    def body(n_ref, *refs):
        c_refs, g_ref, l_ref, e_refs, o_refs, all_ref, x_ref = (
            refs[:4],
            refs[4],
            refs[5],
            refs[6:10],
            refs[10:13],
            refs[13],
            refs[14],
        )
        for r in range(4):
            all_ref[r * n : (r + 1) * n] = c_refs[r][...]
        for r in range(4):
            x = mm(all_ref[:, r * q : (r + 1) * q], g_ref[...], TN).astype(BF)
            put_part(o_refs, r, x, slice(0, cols))
        for r in range(4):
            all_ref[r * n : (r + 1) * n] = e_refs[r][...]
        x_ref[...] = mm(l_ref[...], all_ref[...], TN).astype(BF)
        for r in range(4):
            x = x_ref[turned(n_ref[2], r, k)]
            x = jnp.concatenate([x[:, j * c : (j + 1) * c] for j in range(4)], axis=0)
            put_part(o_refs, r, x, slice(cols, cols + c))

    return call(
        body,
        parts_of(q, cols + c),
        *chunks,
        right,
        left,
        *others,
        scalars=scalars,
        scratch=[((4 * n, wide), BF), ((c, wide), BF)],
    )


def row_parts(left, chunks, scalars):
    n, wide = chunks[0].shape
    k = left.shape[1]

    def body(n_ref, l_ref, *refs):
        c_refs, o_refs, all_ref, sum_ref = refs[:4], refs[4:7], refs[7], refs[8]
        for r in range(4):
            all_ref[r * n : (r + 1) * n] = c_refs[r][...]
        sum_ref[...] = mm(l_ref[...], all_ref[...], TN).astype(BF)
        for r in range(4):
            put_part(o_refs, r, sum_ref[turned(n_ref[2], r, k // 4)])

    return call(
        body,
        parts_of(k // 4, wide),
        left,
        *chunks,
        scalars=scalars,
        scratch=[((4 * n, wide), BF), ((k, wide), BF)],
    )


def for_far(pair, got):
    n = pair.shape[0] // 2

    def body(a_ref, b_ref, o_ref):
        o_ref[:n] = (a_ref[n:].astype(F32) + b_ref[:n].astype(F32)).astype(BF)
        o_ref[n:] = (a_ref[:n].astype(F32) + b_ref[n:].astype(F32)).astype(BF)

    return call(body, (pair.shape, BF), pair, got)


def for_near(near, got):
    n = near.shape[0]

    def body(a_ref, b_ref, o_ref):
        o_ref[...] = (a_ref[...].astype(F32) + b_ref[n:].astype(F32)).astype(BF)

    return call(body, (near.shape, BF), near, got)


def finished(own, near, far, dtype=F32):
    n = own.shape[0]

    def body(a_ref, b_ref, c_ref, o_ref):
        o_ref[...] = (
            a_ref[...].astype(F32) + b_ref[...].astype(F32) + c_ref[:n].astype(F32)
        ).astype(dtype)

    return call(body, (own.shape, dtype), own, near, far)


def finished_rows(own, near, far, scalars):
    n, cols = own.shape
    k = n // 4

    def body(n_ref, a_ref, b_ref, c_ref, *refs):
        refs[4][...] = (
            a_ref[...].astype(F32) + b_ref[...].astype(F32) + c_ref[:n].astype(F32)
        ).astype(BF)
        for r in range(4):
            refs[r][...] = refs[4][turned(n_ref[1], r, k)]

    return call(
        body,
        [((k, cols), BF)] * 4,
        own,
        near,
        far,
        scalars=scalars,
        scratch=[((n, cols), BF)],
    )


def finished_pair(own, near, far, scalars):
    n, cols = own.shape
    c = cols // 4
    k = n // 4

    def body(n_ref, a_ref, b_ref, c_ref, *refs):
        x = a_ref[...].astype(F32) + b_ref[...].astype(F32) + c_ref[:n].astype(F32)
        refs[5][...] = x[:, : 3 * c].astype(BF)
        for r in range(4):
            refs[r][...] = refs[5][turned(n_ref[1], r, k)]
        for j in range(4):
            refs[4][:, j * c : (j + 1) * c] = x[j * k : (j + 1) * k, 3 * c :]

    return call(
        body,
        [((k, 3 * c), BF)] * 4 + [((k, 4 * c), F32)],
        own,
        near,
        far,
        scalars=scalars,
        scratch=[((n, 3 * c), BF)],
    )


def finished_in(own, near, far):
    n = own.shape[0]
    k = n - 16

    def body(a_ref, b_ref, c_ref, o_ref, g_ref):
        o_ref[...] = (
            a_ref[:k].astype(F32) + b_ref[:k].astype(F32) + c_ref[:k].astype(F32)
        )
        g_ref[...] = (
            a_ref[k:].astype(F32) + b_ref[k:].astype(F32) + c_ref[k:n].astype(F32)
        )

    return call(body, [((k, own.shape[1]), F32), ((16, own.shape[1]), F32)], own, near, far)


def gate_and_up(chunks, ws):
    n, wide = chunks[0].shape
    cols = ws[0].shape[1]
    ff = cols // 2
    sizes = [x.shape[0] for x in ws]

    def body(*refs):
        c_refs, w_refs = refs[:4], refs[4 : 4 + len(ws)]
        w_ref, h_ref, a_ref, b_ref, all_ref, x_ref = refs[4 + len(ws) :]
        at = 0
        for ref, size in zip(w_refs, sizes):
            w_ref[at : at + size] = ref[...]
            at += size
        for r in range(4):
            all_ref[r * n : (r + 1) * n] = c_refs[r][...]
        x_ref[...] = mm(all_ref[...], w_ref[...])
        for r in range(4):
            rows = slice(r * n, (r + 1) * n)
            gate, up = pair_down(x_ref[rows])
            sig = jax.nn.sigmoid(gate)
            b = gate * sig
            h_ref[rows] = (b * up).astype(BF)
            a_ref[rows] = up * sig * (1.0 + gate * (1.0 - sig))
            b_ref[rows] = b

    return call(
        body,
        [((wide, cols), BF), ((4 * n, ff), BF), ((4 * n, ff), F32), ((4 * n, ff), F32)],
        *chunks,
        *ws,
        scratch=[((4 * n, wide), BF), ((4 * n, cols), F32)],
    )


def pick_chunks(cot, scalars):
    n, wide = cot.shape[1:]

    def body(n_ref, x_ref, *o_refs):
        for r in range(4):
            o_refs[r][...] = x_ref[n_ref[1] ^ r]

    return call(body, [((n, wide), BF)] * 4, cot, scalars=scalars)


def feed_back(chunks, downs, a, b, w, scalars):
    n, wide = chunks[0].shape
    k = downs[0].shape[0]
    ff = 4 * k

    def body(n_ref, *refs):
        c_refs, d_refs = refs[:4], refs[4:8]
        a_ref, b_ref, w_ref, dw_ref, g_ref = refs[8:13]
        p_refs, all_ref, x_ref = refs[13:17], refs[17], refs[18]
        for r in range(4):
            dw_ref[turned(n_ref[2], r, k)] = d_refs[r][...]
            all_ref[r * n : (r + 1) * n] = c_refs[r][...]
        x_ref[...] = mm(all_ref[...], dw_ref[...], NT)
        for r in range(4):
            rows = slice(r * n, (r + 1) * n)
            x = x_ref[rows]
            g_ref[rows] = pair_up(x * a_ref[rows], x * b_ref[rows]).astype(BF)
        all_ref[...] = mm(g_ref[...], w_ref[...], NT).astype(BF)
        for r in range(4):
            p_refs[r][...] = all_ref[r * n : (r + 1) * n]

    return call(
        body,
        [((ff, wide), BF), ((4 * n, 2 * ff), BF)] + [((n, wide), BF)] * 4,
        *chunks,
        *downs,
        a,
        b,
        w,
        scalars=scalars,
        scratch=[((4 * n, wide), BF), ((4 * n, ff), F32)],
    )


def down_parts(hidden, w):
    rows = hidden.shape[0]
    n = rows // 4

    def body(h_ref, w_ref, *p_refs):
        for r in range(4):
            p_refs[r][...] = mm(h_ref[r * n : (r + 1) * n], w_ref[...]).astype(BF)

    return call(body, [((n, w.shape[1]), BF)] * 4, hidden, w)


def proj_rows(keep, got, gain_one, gain_two):
    rows, c = keep.shape

    def body(a_ref, b_ref, g_ref, h_ref, o_ref):
        o_ref[:rows] = (a_ref[...].astype(F32) + b_ref[...].astype(F32)).astype(BF)
        gains = [x[0:1, i * c : (i + 1) * c] for x in (g_ref, h_ref) for i in range(2)]
        o_ref[rows:] = jnp.concatenate(gains + [jnp.zeros((12, c), F32)], axis=0).astype(BF)

    return call(body, ((rows + 16, c), BF), keep, got, gain_one, gain_two)


def context_terms(chunks, ins, scalars):
    n, wide = chunks[0].shape[0] - 16, chunks[0].shape[1]
    c = ins[0].shape[1]
    half = n // 2

    def body(n_ref, *refs):
        c_refs, w_refs, keep_ref, give_ref, w_all, x_ref, all_ref = (
            refs[:4],
            refs[4:8],
            refs[8],
            refs[9],
            refs[10],
            refs[11],
            refs[12],
        )
        mine = pl.multiple_of(n_ref[0] * half, half)
        theirs = pl.multiple_of((1 - n_ref[0]) * half, half)
        for r in range(4):
            w_all[:, r * c : (r + 1) * c] = w_refs[r][:wide]
            all_ref[r * n : (r + 1) * n] = c_refs[r][:n]
        x_ref[...] = mm(all_ref[...], w_all[...]).astype(BF)
        for r in range(4):
            keep_ref[r] = x_ref[pl.ds(r * n + mine, half)]
            give_ref[r] = x_ref[pl.ds(r * n + theirs, half)]

    return call(
        body,
        [((4, half, 4 * c), BF)] * 2,
        *chunks,
        *ins,
        scalars=scalars,
        scratch=[((wide, 4 * c), BF), ((4 * n, 4 * c), BF), ((4 * n, wide), BF)],
    )


def both_terms(keep, got):
    half, feats = keep.shape[1:]

    def body(a_ref, b_ref, *o_refs):
        for r in range(4):
            o_refs[r][...] = (a_ref[r].astype(F32) + b_ref[r].astype(F32)).astype(BF)

    return call(body, [((half, feats), BF)] * 4, keep, got)


def in_parts(chunks, group, scalars):
    n, wide = chunks[0].shape[0] - 16, chunks[0].shape[1]
    c = group.shape[1] // 4

    def body(n_ref, *refs):
        c_refs, g_ref, o_refs, all_ref, hold = refs[:4], refs[4], refs[5:8], refs[8], refs[9]
        for r in range(4):
            all_ref[r * n : (r + 1) * n] = c_refs[r][:n]
        gains = sum(x[n:].astype(F32) for x in c_refs)
        for i in range(4):
            for k in range(2):
                row = gains[2 * k + i // 2 : 2 * k + i // 2 + 1, (i % 2) * c : (i % 2 + 1) * c]
                hold[i, k : k + 1] = row
            hold[i, 2:] = jnp.zeros((14, c), F32)
        x = mm(all_ref[...], g_ref[...], TN).astype(BF)
        for r in range(4):
            below = hold[n_ref[2] ^ r].astype(BF)
            put_part(
                o_refs, r, jnp.concatenate([x[:, r * c : (r + 1) * c], below], axis=0)
            )

    return call(
        body,
        parts_of(wide + 16, c),
        *chunks,
        group,
        scalars=scalars,
        scratch=[((4 * n, wide), BF), ((4, 16, c), F32)],
    )


def add(*parts, dtype=F32):
    def body(*refs):
        refs[-1][...] = total(refs[:-1]).astype(dtype)

    return call(body, (parts[0].shape, dtype), *parts)


def on_device(
    tokens, context, w_in, attn_gain, w_qkv, w_out, ffn_gain, w_gate_up, w_down, cotangent
):
    s = lax.axis_index("stream")
    t = lax.axis_index("t")
    d = lax.axis_index("d1")
    many = lax.axis_size("d2") > 1
    frames = tokens.shape[0]
    wide = tokens.shape[2]
    scalars = jnp.stack([s, t, d]).astype(jnp.int32)

    def near(w, axis=0):
        return lax.all_gather(w, "d2", axis=axis, tiled=True) if many else w

    def near_sum(g, axis=0):
        return lax.psum_scatter(g, "d2", scatter_dimension=axis, tiled=True) if many else g

    tokens = tokens[:, 0]
    cotangent = cotangent[:, 0]

    gains = jnp.concatenate([near(attn_gain[0]), near(ffn_gain[0])])
    some = gains.shape[0]
    in_mine = near(w_in, 1)
    in_mine = jnp.concatenate(
        [in_mine, jnp.pad(gains[None], ((0, 15), (0, in_mine.shape[1] - some)))]
    )
    fly = Flying()
    in_one, in_three = zhop(in_mine, 1), zhop(in_mine, 3)
    parts = pack_context(context, scalars)
    got = {r: hop(parts[r], r) for r in (3, 2, 1)}
    packed = pack_columns(tie(near(w_qkv[0]), parts[0]), 3)
    if 26 in SKIP:
        packed = tie(packed, in_three)
    qkv_mine = lax.all_to_all(packed, "t", 0, 0, tiled=True).reshape(-1, packed.shape[2])
    packed = pack_pairs(tie(near(w_gate_up[0]), qkv_mine))
    gu_mine = lax.all_to_all(packed, "t", 0, 0, tiled=True).reshape(-1, packed.shape[2])
    fly["gu"] = gu_mine
    own = tie(stack4([parts[0], got[1], got[2], got[3]]), qkv_mine)
    other = swap(own)
    in_two = zhop(opt(0, in_three, own), 1)
    ins = [in_mine, in_one, in_two, in_three]
    qkv_mine = beside(qkv_mine, near(w_out[0]))
    fly["qkv1"], fly["qkv3"] = zhop(qkv_mine, 1), zhop(qkv_mine, 3)
    group, parts = project(own, fly.due("group", other), ins, some, scalars)

    parts[0] = fly.due("parts0", parts[0])
    parts = collect(parts)
    proj_half = fly.due("half", half_sum(parts))
    start, mine, gains = first_norm(proj_half, swap(proj_half), parts, tokens, scalars)
    mine = fly.due("mine1", mine)
    by_x, by_y = hop(mine, 1), hop(mine, 2)
    fly["qkv2"] = zhop(opt(1, fly["qkv3"], mine), 1)
    by_y = fly.due("byy1", by_y)
    by_xy = corner(30, by_y, mine)
    gu_mine = opt(2, gu_mine, by_y)
    upper, lower = gu_mine[: gu_mine.shape[0] // 2], gu_mine[gu_mine.shape[0] // 2 :]
    whole = 37 in SKIP
    fly["gu1"], fly["up3"] = zhop(gu_mine, 1), zhop(gu_mine if whole else upper, 3)
    ws = [qkv_mine, fly["qkv1"], fly["qkv2"], fly["qkv3"]]
    chunks_one = [mine, by_x, by_y, fly.due("byxy1", by_xy)]
    q, kv, qkv_w = query_key_value(chunks_one, ws)
    if 36 in SKIP:
        cot = opt(3, cotangent, q)
        fly["coty"], fly["cotx"] = hop(cot, 2), hop(cot, 1)
    else:
        fly["cot"] = lax.all_to_all(
            jnp.broadcast_to(opt(3, cotangent, q)[None], (4, frames, wide)), "t", 0, 0, tiled=True
        )
    far = lax.ppermute(fly.due("kv", kv), "stream", [(0, 1)])
    if not whole:
        fly["low3"] = zhop(opt(4, lower, q), 3)
    mixed, w_own, out_w, *parts = attend(q, kv, far, ws, scalars)
    fly["up2"] = zhop(opt(5, fly["up3"], mixed), 1)
    parts[0] = fly.due("parts1", parts[0])
    parts = collect(parts)
    parts[0] = fly.due("mid", parts[0])
    middle, mine = second_norm(start, parts, gains, scalars)
    if not whole:
        fly["low2"] = zhop(opt(6, fly["low3"], middle), 1)
    if 36 in SKIP:
        fly["cotxy"] = corner(38, opt(39, fly["coty"], middle), cot)
    down_mine = near(w_down[0])
    fly["down1"] = zhop(opt(7, down_mine, middle), 1)

    mine = fly.due("mine2", mine)
    by_x, by_y = hop(mine, 1), hop(mine, 2)
    by_y = fly.due("byy2", by_y)
    by_xy = corner(31, by_y, mine)
    fly["down3"] = zhop(opt(8, down_mine, mine), 3)
    chunks_two = [mine, by_x, by_y, fly.due("byxy2", by_xy)]
    gus = [gu_mine, fly["gu1"], fly["up2"], fly["up3"]]
    if not whole:
        gus = [gu_mine, fly["gu1"], fly["up2"], fly["low2"], fly["up3"], fly["low3"]]
    gu_w, hidden, a, b = gate_and_up(chunks_two, gus)
    fly["down2"] = zhop(opt(9, fly["down3"], by_xy), 1)
    hidden = fly.due("hidden", hidden)
    if 36 in SKIP:
        cot = [cot, fly["cotx"], fly["coty"], fly["cotxy"]]
    else:
        cot = pick_chunks(fly["cot"].reshape(4, frames, wide), scalars)
    g = row_parts(hidden, cot, scalars)
    far_g = inward(opt(10, g[2], fly["down2"]))
    fly["g1"] = far_g
    downs = [down_mine, fly["down1"], fly["down2"], fly["down3"]]
    down_w, grad_gu, *parts = feed_back([opt(11, cot[0], g[0])] + cot[1:], downs, a, b, gu_w, scalars)
    u = weight_parts(chunks_two, opt(12, grad_gu, parts[0]))
    far_u = inward(u[2])
    fly["u1"] = far_u
    parts[0] = fly.due("parts2", parts[0])
    parts = collect(parts)
    parts[0] = fly.due("nb2", parts[0])
    far_g = across(for_far(g[2], opt(13, far_g, parts[0])))
    fly["g2"] = far_g
    grad_middle, gain_two, mine = norm_back(
        parts, middle, gains, 1, cotangent, scalars, False
    )
    mine = fly.due("mine3", mine)
    branch = [mine, hop(mine, 1), hop(mine, 2)]
    branch[2] = fly.due("byy3", branch[2])
    branch.append(fly.due("branch", corner(32, branch[2], mine)))
    near_g = zhop(for_near(g[1], opt(14, far_g, branch[3])), 1)
    fly["g3"] = near_g

    grad, back = attend_back(branch, out_w, w_own, q, kv, far)
    back = lax.ppermute(fly.due("back", back), "stream", [(1, 0)])
    parts = collect(down_parts(opt(15, hidden, branch[3]), down_w))
    result = add(middle, *parts)
    fly["result"] = result
    far_u = across(for_far(u[2], opt(16, far_u, back)))
    fly["u2"] = far_u
    grad_qkv, *parts = into_normed(grad, fly.due("into", back), qkv_w)
    parts[0] = fly.due("parts3", parts[0])
    h = attention_parts(chunks_one, opt(17, grad_qkv, parts[0]), mixed, branch, scalars)
    far_h = inward(h[2])
    fly["h1"] = far_h
    parts = collect(parts)
    parts[0] = fly.due("nb1", parts[0])
    grad_start, gain_one, keep, give = norm_back(
        parts, start, gains, 0, grad_middle, scalars, True
    )
    grad_proj = proj_rows(fly.due("keep", keep), swap(give), gain_one, gain_two)
    far_h = across(for_far(h[2], opt(18, far_h, grad_proj)))
    fly["h2"] = far_h
    gproj = [grad_proj, hop(grad_proj, 1), hop(grad_proj, 2)]
    gproj[2] = fly.due("gpy", gproj[2])
    gproj.append(fly.due("gproj", corner(33, gproj[2], grad_proj)))
    near_u = zhop(for_near(u[1], opt(19, far_u, gproj[3])), 1)
    fly["u3"] = near_u

    g_in = in_parts(gproj, group, scalars)
    far_in = inward(g_in[2])
    fly["in1"] = far_in
    keep, give = context_terms([opt(20, gproj[0], g_in[0])] + gproj[1:], ins, scalars)
    both = both_terms(keep, fly.due("both", swap(fly.due("give", give))))
    got = [both[0]] + [hop(both[r], r) for r in (1, 2, 3)]
    got = fly.due("got", stack4(got))
    blocks = finished_rows(u[0], near_u, opt(21, far_u, got), scalars)
    g_gu = [blocks[0]] + [hop(blocks[r], r) for r in (1, 2, 3)]
    far_in = across(for_far(g_in[2], opt(22, far_in, got)))
    fly["in2"] = far_in
    near_h = zhop(for_near(h[1], opt(23, far_h, got)), 1)
    fly["h3"] = near_h
    other = swap(got)
    g_gu[0] = fly.due("gu_out", g_gu[0])
    grad_gate_up = unpack_columns(g_gu, 2, scalars)
    near_in = zhop(for_near(g_in[1], opt(24, far_in, grad_gate_up)), 1)
    fly["in3"] = near_in
    *blocks, grad_out = finished_pair(h[0], near_h, opt(25, far_h, grad_gate_up), scalars)
    g_qkv = [blocks[0]] + [hop(blocks[r], r) for r in (1, 2, 3)]
    grad_context = unpack_context(got, fly.due("context", other), scalars)
    grad_gate_up = near_sum(grad_gate_up)
    grad_qkv = near_sum(unpack_columns(g_qkv, 3, scalars))
    grad_out = near_sum(grad_out)
    grad_down = near_sum(finished(g[0], near_g, fly["g2"]))
    grad_in, found = finished_in(g_in[0], near_in, far_in)
    grad_in = near_sum(grad_in, 1)
    found = lax.dynamic_slice_in_dim(found[:2], t * (some // 2), some // 2, 1)
    gains = near_sum(found, 1)
    return (
        result[:, None],
        grad_start[:, None],
        grad_context,
        grad_in,
        gains[:1],
        grad_qkv[None],
        grad_out[None],
        gains[1:],
        grad_gate_up[None],
        grad_down[None],
    )


def solution(mesh):
    n = mesh.shape["frames"]
    grid = Mesh(mesh.devices.reshape(2, 4, 4, n // 16), ("stream", "d1", "t", "d2"))
    f = ("d1", "t", "d2")
    return jax.shard_map(
        on_device,
        mesh=grid,
        in_specs=(
            P(f, "stream", None),
            P(f, None),
            P("stream", f),
            P("stream", f),
            P("stream", f, None),
            P("stream", f, None),
            P("stream", f),
            P("stream", f, None),
            P("stream", f, None),
            P(f, "stream", None),
        ),
        out_specs=(
            P(f, "stream", None),
            P(f, "stream", None),
            P(f, None),
            P("stream", f),
            P("stream", f),
            P("stream", f, None),
            P("stream", f, None),
            P("stream", f),
            P("stream", f, None),
            P("stream", f, None),
        ),
        check_vma=False,
    )
```
